32 devices in a mesh: mem: 4 (over y, x), grid: 8 (over z, core).
Axes of the slice: x: 2, y: 2, z: 4, core: 2. Of those that a mesh axis runs over, the one named last changes fastest.
Arguments:
- initial_concentrations: float32 [16, 4, 768, 1536], P('mem', None, 'grid'), may hold values from 0.5 to 2
- rate_field: bfloat16 [12, 768, 1536], P(None, 'grid'), may hold values from 0.019897461 to 0.29882812
- kinetic_scaling_factors: bfloat16 [16, 12, 256, 6], P('mem', None, 'grid'), may hold values from 0.5 to 2
- observed_cell: int32 [256, 6, 128], P('grid'), may hold values from 0 to 3071
- measured_value: float32 [256, 6, 128], P('grid'), may hold values from 0.5 to 2
- error_variance: float32 [256, 6, 128], P('grid'), may hold values from 0.05 to 0.5
Outputs:
- analysis: bfloat16 [16, 4, 768, 1536], P('mem', None, 'grid')
- mult_analysis: bfloat16 [16, 12, 256, 6], P('mem', None, 'grid')
The draws below stay inside these ranges and needn't reach their ends.
Inputs may be any that keep to these rules, and one draw needn't show every extreme that they name: `observed_cell`: an observation's entry is tracer * 3 * 256 + row * 256 + column within its patch.
All inputs are finite; a program needn't handle non-finite values.
Results may differ from the reference program's by a relative error of at most 0.011.
The reference program's roundings to bfloat16 on the way count: a program that leaves them out, or rounds other values in their place, can miss the bound.
Values may be sent and summed in bfloat16 or wider, within the bound.
No kernel may reach another device: no remote copies, remote signals or barrier semaphores. Data moves between devices by JAX's collectives and lax.ppermute only.
A program may use at most 192 MiB of HBM per device.

```python
import math
import jax
import jax.numpy as jnp
from jax import lax

NLAT = 768
NLON = 1536
NW = 512
TRACERS = 4
STEPS = 1
PLAT = 3
PLON = 256
SWEEPS = 5
OBS = 128
REACTIONS = 12
M = 16
NPY = 256
NPX = 6


def with_ends(array, own_key, low, high):
    longest = array.shape.index(max(array.shape))
    spots = []
    for shift in (0, 1):
        where = [jax.random.randint(jax.random.fold_in(own_key, axis), (), 0, length) for axis, length in enumerate(array.shape)]
        where[longest] = (where[longest] + shift) % array.shape[longest]
        spots.append(tuple(where))
    return array.at[spots[0]].set(low).at[spots[1]].set(high)


def block_scale(own_key, shape, split, smallest, top_value):
    def one(axis_at, parts):
        steps = jax.random.uniform(jax.random.fold_in(jax.random.fold_in(own_key, 6), axis_at), (parts,), jnp.float32, smallest / len(split), top_value / len(split))
        return jnp.repeat(jnp.exp(steps), shape[axis_at] // parts).reshape((-1,) + (1,) * (len(shape) - axis_at - 1))

    loudness = one(*split[0])
    for cut in split[1:]:
        loudness = loudness * one(*cut)
    return loudness


def setup_inputs(seed: int = 0) -> dict:
    key_list = jax.random.split(jax.random.key(seed), 7)
    initial_concentrations = jnp.clip(0.5 + 1.5 * jax.random.uniform(key_list[0], (M, TRACERS, NLAT, NLON), jnp.float32) ** block_scale(key_list[0], (M, TRACERS, NLAT, NLON), ((0, 4), (2, 8)), -0.2, 0.2), 0.5, 2.0)
    rate_field = jnp.clip(jnp.exp(math.log(0.29882812) - 2.7092764 * jax.random.uniform(key_list[1], (REACTIONS, NLAT, NLON), jnp.float32) ** block_scale(key_list[1], (REACTIONS, NLAT, NLON), ((1, 8),), -0.2, 0.2)), 0.019897461, 0.29882812).astype(jnp.bfloat16)
    kinetic_scaling_factors = jnp.clip(jnp.exp(math.log(2.0) - 1.3862944 * jax.random.uniform(key_list[2], (M, REACTIONS, NPY, NPX), jnp.float32) ** block_scale(key_list[2], (M, REACTIONS, NPY, NPX), ((0, 4), (2, 8)), -0.2, 0.2)), 0.5, 2.0).astype(jnp.bfloat16)
    observed_cell = with_ends(jax.random.randint(key_list[3], (NPY, NPX, OBS), 0, TRACERS * PLAT * PLON), jax.random.fold_in(key_list[3], 1), 0, (TRACERS * PLAT * PLON) - 1).astype(jnp.int32)
    measured_value = jnp.clip(0.5 + 1.5 * jax.random.uniform(key_list[4], (NPY, NPX, OBS), jnp.float32) ** block_scale(key_list[4], (NPY, NPX, OBS), ((0, 8),), -0.2, 0.2), 0.5, 2.0)
    error_variance = jnp.clip(jnp.exp(math.log(0.5) - 2.3025851 * jax.random.uniform(key_list[5], (NPY, NPX, OBS), jnp.float32) ** block_scale(key_list[5], (NPY, NPX, OBS), ((0, 8),), -0.2, 0.2)), 0.05, 0.5)
    return dict(initial_concentrations=initial_concentrations, rate_field=rate_field, kinetic_scaling_factors=kinetic_scaling_factors, observed_cell=observed_cell, measured_value=measured_value, error_variance=error_variance)


damping = 2.0

def zonal_lookup(longitudes, wavenumbers):
    column = jnp.arange(longitudes, dtype=jnp.int32)
    wave = jnp.arange(wavenumbers, dtype=jnp.int32)
    phase = wave[:, None] * column[None, :] % longitudes
    angle = phase.astype(jnp.float32) * (2.0 * math.pi / longitudes)
    cosine = jnp.cos(angle)
    sine = jnp.sin(angle)
    forward = jnp.stack([cosine, -sine], axis=1).reshape(2 * wavenumbers, longitudes).T.astype(jnp.bfloat16)
    weight = jnp.where(wave == 0, 1.0, 2.0).astype(jnp.float32)[:, None]
    inverse = jnp.stack([weight * cosine, -weight * sine], axis=1).reshape(2 * wavenumbers, longitudes).astype(jnp.bfloat16)
    return (forward, inverse)

def meridional_table(wave_ids, latitudes, wavenumbers):
    modes = jnp.arange(wavenumbers, dtype=jnp.int32)
    theta = (jnp.arange(latitudes, dtype=jnp.float32) + 0.5) * (math.pi / latitudes)
    order = modes.astype(jnp.float32)
    cosine = jnp.cos(theta[:, None] * order[None, :])
    sine = jnp.sin(theta[:, None] * (order[None, :] + 1.0))
    even = (wave_ids % 2 == 0)[:, None, None]
    kept = (modes[None, :] + wave_ids[:, None] <= wavenumbers - 1)[:, None, :]
    return jnp.where(kept, jnp.where(even, cosine[None], sine[None]), 0.0).astype(jnp.bfloat16)

def spectral_gain(wave_ids, wavenumbers):
    modes = jnp.arange(wavenumbers, dtype=jnp.int32)
    total = (wave_ids[:, None] + modes[None, :]).astype(jnp.float32)
    ratio = total * (total + 1.0) / float(wavenumbers * (wavenumbers - 1))
    half = jnp.where((wave_ids[:, None] % 2 == 0) & (modes[None, :] == 0), 0.5, 1.0)
    return (half / (1.0 + damping * ratio * ratio)).astype(jnp.float32)

def local_rates(factors, photolysis, patch_rows, patch_cols):
    reactions, rows, cols = photolysis.shape
    shaped = photolysis.astype(jnp.float32).reshape(reactions, rows // patch_rows, patch_rows, cols // patch_cols, patch_cols)
    scaled = factors.astype(jnp.float32)[..., :, :, None, :, None] * shaped
    return scaled.reshape(factors.shape[:-2] + (rows, cols))

def react(tracer_amounts, rates):
    count = tracer_amounts.shape[-3]
    others = count - 1
    leave = []
    for source in range(count):
        outflow = rates[..., others * source, :, :]
        for turn in range(1, others):
            outflow = outflow + rates[..., others * source + turn, :, :]
        leave.append(1.0 / (1.0 + outflow))
    result = []
    for target in range(count):
        value = tracer_amounts[..., target, :, :] * leave[target]
        for source in range(count):
            if source != target:
                turn = target if target < source else target - 1
                value = value + rates[..., others * source + turn, :, :] * leave[source] * tracer_amounts[..., source, :, :]
        result.append(value)
    return jnp.stack(result, axis=-3)

def ensemble_update(patches, theta, positions, observed, variance):
    highest = lax.Precision.HIGHEST
    members = patches.shape[1]
    values = patches.astype(jnp.float32)
    midpoint = lax.optimization_barrier(jnp.mean(values, axis=1, keepdims=True))
    perturbation = values - midpoint
    index_full = jnp.broadcast_to(positions[:, None, :], (positions.shape[0], members, positions.shape[1]))
    predicted = jnp.take_along_axis(values, index_full, axis=2)
    seen_mean = lax.optimization_barrier(jnp.mean(predicted, axis=1, keepdims=True))
    seen_spread = predicted - seen_mean
    weighted = seen_spread * (1.0 / variance)[:, None, :]
    outer = jnp.einsum('pik,pjk->pij', weighted, seen_spread, precision=highest)
    scale = members - 1.0 + jnp.sqrt(lax.optimization_barrier(jnp.sum(outer * outer, axis=(1, 2))))
    identity = jnp.eye(members, dtype=jnp.float32)
    current = ((members - 1.0) * identity + outer) / scale[:, None, None]
    root = jnp.broadcast_to(identity, current.shape)
    for sweep in range(SWEEPS):
        middle = 1.5 * identity - 0.5 * jnp.einsum('pij,pjk->pik', root, current, precision=highest)
        current = jnp.einsum('pij,pjk->pik', current, middle, precision=highest)
        root = jnp.einsum('pij,pjk->pik', middle, root, precision=highest)
    covariance = jnp.einsum('pij,pjk->pik', root, root, precision=highest) / scale[:, None, None]
    innovation = observed - seen_mean[:, 0, :]
    projected = jnp.einsum('pjk,pk->pj', weighted, innovation, precision=highest)
    average_coefficient = jnp.einsum('pij,pj->pi', covariance, projected, precision=highest)
    transform = jnp.sqrt((members - 1.0) / scale)[:, None, None] * root + average_coefficient[:, :, None]
    analysis = midpoint + jnp.einsum('pik,pij->pjk', perturbation, transform, precision=highest)
    theta_mean = lax.optimization_barrier(jnp.mean(theta, axis=1, keepdims=True))
    theta_new = theta_mean + jnp.einsum('pir,pij->pjr', theta - theta_mean, transform, precision=highest)
    return (analysis.astype(jnp.bfloat16), jnp.exp(theta_new).astype(jnp.bfloat16))

def reference(initial_concentrations, rate_field, kinetic_scaling_factors, observed_cell, measured_value, error_variance):
    forward, inverse = zonal_lookup(NLON, NW)
    block = min(NW, 64)

    def one_block(bundled_realizations):
        piece, first = bundled_realizations
        wave_ids = first + jnp.arange(block, dtype=jnp.int32)
        table = meridional_table(wave_ids, NLAT, NW).astype(jnp.float32)
        gain = spectral_gain(wave_ids, NW)
        spectrum = jnp.einsum('fjmc,mjk->fmck', piece.astype(jnp.float32), table) * (2.0 / NLAT)
        damped = (spectrum * gain[None, :, None, :]).astype(jnp.bfloat16)
        back = jnp.einsum('fmck,mjk->fjmc', damped.astype(jnp.float32), table)
        return back.astype(jnp.bfloat16)

    def meridional(fourier):
        pieces = fourier.reshape(TRACERS, NLAT, NW // block, block, 2).transpose(2, 0, 1, 3, 4)
        firsts = jnp.arange(NW // block, dtype=jnp.int32) * block
        backs = lax.map(one_block, (pieces, firsts))
        return backs.transpose(1, 2, 0, 3, 4).reshape(TRACERS, NLAT, 2 * NW)

    def predicted_concentration(bundled_realizations):
        tracer_amounts, factors = bundled_realizations
        rates = local_rates(factors, rate_field, PLAT, PLON)
        for step in range(STEPS):
            flat = tracer_amounts.astype(jnp.bfloat16).reshape(TRACERS * NLAT, NLON)
            fourier = (jnp.dot(flat, forward, preferred_element_type=jnp.float32) * (1.0 / NLON)).astype(jnp.bfloat16)
            back = meridional(fourier.reshape(TRACERS, NLAT, NW, 2))
            smooth = jnp.dot(back.reshape(TRACERS * NLAT, 2 * NW), inverse, preferred_element_type=jnp.float32)
            tracer_amounts = react(smooth.reshape(TRACERS, NLAT, NLON), rates)
        return tracer_amounts.astype(jnp.bfloat16)
    background_concentrations = lax.map(predicted_concentration, (initial_concentrations, kinetic_scaling_factors))
    rows_count = NLAT // PLAT
    cols_count = NLON // PLON
    cells = TRACERS * PLAT * PLON
    patches = background_concentrations.reshape(M, TRACERS, rows_count, PLAT, cols_count, PLON).transpose(2, 4, 0, 1, 3, 5).reshape(rows_count, cols_count, M, cells)
    theta = jnp.log(kinetic_scaling_factors.astype(jnp.float32)).transpose(2, 3, 0, 1)

    def one_row(bundled_realizations):
        row_patches, row_theta, row_cells, row_values, line_dispersion = bundled_realizations
        return ensemble_update(row_patches, row_theta, row_cells, row_values, line_dispersion)
    new_rows, new_rates = lax.map(one_row, (patches, theta, observed_cell, measured_value, error_variance))
    analysis = new_rows.reshape(rows_count, cols_count, M, TRACERS, PLAT, PLON).transpose(2, 3, 0, 4, 1, 5).reshape(M, TRACERS, NLAT, NLON)
    mult_analysis = new_rates.transpose(2, 3, 0, 1)
    return (analysis, mult_analysis)
```

```python
import functools
import math

import jax
import jax.numpy as jnp
from jax import lax
from jax.experimental import pallas as pl
from jax.experimental.pallas import tpu as pltpu
from jax.sharding import PartitionSpec as P

NW = 512
PLAT = 3
PLON = 256
SWEEPS = 5
LANES = 128
SUBLANES = 8

damping = 2.0
f32 = jnp.float32
bf16 = jnp.bfloat16


def rounded_angle(product, period):
    turns = jnp.floor(product * (1.0 / period))
    return (product - turns * period) * (2.0 * math.pi / period)


def forward_kernel(bands, waves, x_ref, o_ref, table, coarse, fine):
    tracers, band, longitudes = x_ref.shape[1:]
    columns = table.shape[1]
    local = 2 * waves
    step = fine.shape[1]

    @pl.when(pl.program_id(0) == 0)
    def _():
        def waves_of(rows):
            q = lax.broadcasted_iota(jnp.int32, (rows, columns), 1)
            p = q // local
            part = (q % local) // waves
            wave = bands * (q % waves) + p
            return wave.astype(f32), part

        rows = coarse.shape[1]
        wave, part = waves_of(rows)
        row = lax.broadcasted_iota(jnp.int32, (rows, columns), 0) * step
        angle = rounded_angle(wave * row.astype(f32), longitudes)
        cosine, sine = jnp.cos(angle), jnp.sin(angle)
        coarse[0] = jnp.where(part == 0, cosine, -sine)
        coarse[1] = jnp.where(part == 0, sine, cosine)
        wave, part = waves_of(step)
        row = lax.broadcasted_iota(jnp.int32, (step, columns), 0)
        angle = rounded_angle(wave * row.astype(f32), longitudes)
        fine[0] = jnp.cos(angle)
        fine[1] = jnp.sin(angle)

        def build(at, carry):
            block = coarse[0, pl.ds(at, 1), :] * fine[0] - coarse[1, pl.ds(at, 1), :] * fine[1]
            start = pl.multiple_of(at * step, step)
            table[pl.ds(start, step), :] = block.astype(bf16)
            return carry

        lax.fori_loop(0, rows, build, 0)

    x = x_ref[0].astype(bf16).reshape(tracers * band, longitudes)
    y = jnp.dot(x, table[...], preferred_element_type=f32) * (1.0 / longitudes)
    y = y.astype(bf16).reshape(tracers, band, columns)
    for t in range(tracers):
        for p in range(bands):
            o_ref[p, :, t * local : (t + 1) * local] = y[t, :, p * local : (p + 1) * local]


def forward_transform(x, bands, waves):
    group, tracers, band, longitudes = x.shape
    local = 2 * waves
    step = 32 if longitudes % 32 == 0 else 8
    return pl.pallas_call(
        functools.partial(forward_kernel, bands, waves),
        grid=(group,),
        in_specs=[pl.BlockSpec((1, tracers, band, longitudes), lambda g: (g, 0, 0, 0))],
        out_specs=pl.BlockSpec((bands, band, tracers * local), lambda g: (0, 0, g)),
        out_shape=jax.ShapeDtypeStruct((bands, band, group * tracers * local), bf16),
        scratch_shapes=[
            pltpu.VMEM((longitudes, bands * local), bf16),
            pltpu.VMEM((2, longitudes // step, bands * local), f32),
            pltpu.VMEM((2, step, bands * local), f32),
        ],
        compiler_params=pltpu.CompilerParams(vmem_limit_bytes=60 * 2**20),
        name="forward_dft",
    )(x)


def meridional_kernel(waves, a_ref, ahead_ref, back_ref, gain_ref, o_ref):
    local = 2 * waves
    tracers = a_ref.shape[1] // local
    spectrum = jnp.dot(ahead_ref[...], a_ref[...], preferred_element_type=f32)
    gain = jnp.concatenate([gain_ref[...]] * tracers, axis=1)
    damped = (spectrum * gain).astype(bf16)
    back = jnp.dot(back_ref[...], damped, preferred_element_type=f32).astype(bf16)
    owners, _, rows, _ = o_ref.shape
    own = rows // tracers
    for t in range(tracers):
        part = back[:, t * local : (t + 1) * local].reshape(owners, own, local)
        o_ref[:, 0, t * own : (t + 1) * own, :] = part


def meridional_transform(arrived, ahead, back, gain, waves, tracers, owners):
    latitudes, columns = arrived.shape
    local = 2 * waves
    group = columns // (tracers * local)
    own = latitudes // owners
    whole = lambda g: (0, 0)
    return pl.pallas_call(
        functools.partial(meridional_kernel, waves),
        grid=(group,),
        in_specs=[
            pl.BlockSpec((latitudes, tracers * local), lambda g: (0, g)),
            pl.BlockSpec(ahead.shape, whole),
            pl.BlockSpec(back.shape, whole),
            pl.BlockSpec(gain.shape, whole),
        ],
        out_specs=pl.BlockSpec((owners, 1, tracers * own, local), lambda g: (0, g, 0, 0)),
        out_shape=jax.ShapeDtypeStruct((owners, group, tracers * own, local), bf16),
        compiler_params=pltpu.CompilerParams(vmem_limit_bytes=60 * 2**20),
        name="meridional",
    )(arrived, ahead, back, gain)


def meridional_tables(latitudes, own, bands, groups):
    device = lax.axis_index("grid")
    even = device % 2 == 0
    modes = jnp.arange(NW, dtype=jnp.int32)
    order = jnp.where(even, modes, modes + 1).astype(f32)

    def values(theta, order):
        angle = theta * order
        return jnp.where(even, jnp.cos(angle), jnp.sin(angle)).astype(bf16)

    theta = (jnp.arange(latitudes, dtype=f32) + 0.5) * (math.pi / latitudes)
    ahead = values(theta[None, :], order[:, None])
    rows = own // PLAT
    index = (
        lax.broadcasted_iota(jnp.int32, (groups, bands, PLAT, rows), 0) * own
        + lax.broadcasted_iota(jnp.int32, (groups, bands, PLAT, rows), 1) * (own * groups)
        + lax.broadcasted_iota(jnp.int32, (groups, bands, PLAT, rows), 2)
        + lax.broadcasted_iota(jnp.int32, (groups, bands, PLAT, rows), 3) * PLAT
    ).reshape(latitudes)
    theta = (index.astype(f32) + 0.5) * (math.pi / latitudes)
    back = values(theta[:, None], order[None, :])
    return ahead, back


def spectral_gain(latitudes, waves, bands):
    device = lax.axis_index("grid")
    modes = jnp.arange(NW, dtype=jnp.int32)[:, None]
    column = jnp.arange(2 * waves, dtype=jnp.int32)[None, :]
    wave = bands * (column % waves) + device
    total = (wave + modes).astype(f32)
    ratio = total * (total + 1.0) / float(NW * (NW - 1))
    half = jnp.where((wave % 2 == 0) & (modes == 0), 0.5, 1.0)
    gain = half / (1.0 + damping * ratio * ratio)
    return jnp.where(wave + modes <= NW - 1, gain, 0.0) * (2.0 / latitudes)


def inverse_table(longitudes, waves, bands):
    q = jnp.arange(bands * 2 * waves, dtype=jnp.int32)
    device = q // (2 * waves)
    part = (q % (2 * waves)) // waves
    wave = bands * (q % waves) + device
    column = jnp.arange(longitudes, dtype=jnp.int32)
    phase = wave[:, None] * column[None, :] % longitudes
    phase = phase + jnp.where(part == 0, 0, longitudes // 4)[:, None]
    weight = jnp.where(wave == 0, 1.0, 2.0)[:, None]
    angle = phase.astype(f32) * (2.0 * math.pi / longitudes)
    return (weight * jnp.cos(angle)).astype(bf16)


def chemistry_kernel(
    z_ref, table_ref, rate_ref, factor_ref, lane_ref, place_ref, bg_ref, seen_ref, lhs, smooth, fresh
):
    sources, bands, rows, local = z_ref.shape
    reactions, height, patch_rows, _ = rate_ref.shape
    members = factor_ref.shape[1]
    tracers = bg_ref.shape[0]
    others = tracers - 1
    group = members // sources
    own = height * patch_rows

    @pl.when(pl.program_id(0) == 0)
    def _():
        for s in range(sources):
            for p in range(bands):
                lhs[s * rows : (s + 1) * rows, p * local : (p + 1) * local] = z_ref[s, p]

    smooth[...] = jnp.dot(lhs[...], table_ref[...], preferred_element_type=f32).reshape(
        members, tracers, height, patch_rows, PLON
    )

    def one_member(e, carry):
        for i in range(height):
            for at in range(0, PLON, LANES):
                lanes = slice(at, at + LANES)
                rates = [
                    factor_ref[0, e, r] * rate_ref[r, i, :, lanes] for r in range(reactions)
                ]
                moved, kept = [], []
                for a in range(tracers):
                    outflow = rates[others * a]
                    for s in range(1, others):
                        outflow = outflow + rates[others * a + s]
                    kept.append(smooth[e, a, i, :, lanes] * (1.0 / (1.0 + outflow)))
                for b in range(tracers):
                    value = kept[b]
                    for a in range(tracers):
                        if a != b:
                            s = b if b < a else b - 1
                            value = value + rates[others * a + s] * kept[a]
                    fresh[b, i, e, :, lanes] = value
        return carry

    lax.fori_loop(0, members, one_member, 0)
    for t in range(tracers):
        for i in range(height):
            bg_ref[t, i] = fresh[t, i].reshape(members * patch_rows, PLON).astype(bf16)

    copies = max(1, SUBLANES // patch_rows)

    def tiled(array):
        return jnp.concatenate([array] * copies, axis=0) if copies > 1 else array

    lane = tiled(lane_ref[0])
    place = tiled(place_ref[0])
    within = lane % LANES
    piece = lane // LANES

    def observe(e, carry):
        seen = jnp.zeros(lane.shape, f32)
        for t in range(tracers):
            for i in range(height):
                value = tiled(fresh[t, i, e])
                for k in range(PLON // LANES):
                    found = jnp.take_along_axis(
                        value[:, k * LANES : (k + 1) * LANES],
                        within,
                        axis=1,
                        mode="promise_in_bounds",
                    )
                    here = (place == t * height + i) & (piece == k)
                    seen = jnp.where(here, found, seen)
        seen_ref[0, e] = seen[:patch_rows].astype(bf16).astype(f32)
        return carry

    lax.fori_loop(0, members, observe, 0)


def chemistry(z, table, rate, factor, lane, place, tracers):
    sources, bands, rows, local = z.shape
    reactions, height, patch_rows, longitudes = rate.shape
    cols, members = factor.shape[:2]
    observations = lane.shape[-1]
    return pl.pallas_call(
        chemistry_kernel,
        grid=(cols,),
        in_specs=[
            pl.BlockSpec(z.shape, lambda c: (0, 0, 0, 0)),
            pl.BlockSpec((table.shape[0], PLON), lambda c: (0, c)),
            pl.BlockSpec((reactions, height, patch_rows, PLON), lambda c: (0, 0, 0, c)),
            pl.BlockSpec((1, members, reactions, patch_rows, LANES), lambda c: (c, 0, 0, 0, 0)),
            pl.BlockSpec((1, patch_rows, observations), lambda c: (c, 0, 0)),
            pl.BlockSpec((1, patch_rows, observations), lambda c: (c, 0, 0)),
        ],
        out_specs=[
            pl.BlockSpec((tracers, height, members * patch_rows, PLON), lambda c: (0, 0, 0, c)),
            pl.BlockSpec((1, members, patch_rows, observations), lambda c: (c, 0, 0, 0)),
        ],
        out_shape=[
            jax.ShapeDtypeStruct((tracers, height, members * patch_rows, longitudes), bf16),
            jax.ShapeDtypeStruct((cols, members, patch_rows, observations), f32),
        ],
        scratch_shapes=[
            pltpu.VMEM((sources * rows, bands * local), bf16),
            pltpu.VMEM((members, tracers, height, patch_rows, PLON), f32),
            pltpu.VMEM((tracers, height, members, patch_rows, PLON), f32),
        ],
        compiler_params=pltpu.CompilerParams(vmem_limit_bytes=60 * 2**20),
        name="chemistry",
    )(z, table, rate, factor, lane, place)


def apply_kernel(high_ref, low_ref, bg_ref, o_ref, rows):
    members, tracers, own, _ = o_ref.shape
    height = bg_ref.shape[1]
    patch_rows = own // height
    for t in range(tracers):
        for i in range(height):
            value = bg_ref[t, i]
            new = jnp.dot(high_ref[0], value, preferred_element_type=f32)
            new = new + jnp.dot(low_ref[0], value, preferred_element_type=f32)
            for j in range(members):
                part = new[j * patch_rows : (j + 1) * patch_rows]
                for k in range(PLON // LANES):
                    rows[k, j, pl.ds(i, patch_rows, stride=height), :] = part[
                        :, k * LANES : (k + 1) * LANES
                    ]
        for k in range(PLON // LANES):
            o_ref[:, t, :, k * LANES : (k + 1) * LANES] = rows[k].astype(bf16)


def apply_weights(high, low, bg, members, own):
    tracers, height, wide, longitudes = bg.shape
    cols = high.shape[0]
    return pl.pallas_call(
        apply_kernel,
        grid=(cols,),
        in_specs=[
            pl.BlockSpec((1, wide, wide), lambda c: (c, 0, 0)),
            pl.BlockSpec((1, wide, wide), lambda c: (c, 0, 0)),
            pl.BlockSpec((tracers, height, wide, PLON), lambda c: (0, 0, 0, c)),
        ],
        out_specs=pl.BlockSpec((members, tracers, own, PLON), lambda c: (0, 0, 0, c)),
        out_shape=jax.ShapeDtypeStruct((members, tracers, own, longitudes), bf16),
        scratch_shapes=[pltpu.VMEM((PLON // LANES, members, own, LANES), f32)],
        compiler_params=pltpu.CompilerParams(vmem_limit_bytes=60 * 2**20),
        name="apply_weights",
    )(high, low, bg)


def ensemble_transform(predicted, observed, variance):
    highest = lax.Precision.HIGHEST
    members = predicted.shape[1]
    seen_mean = jnp.mean(predicted, axis=1, keepdims=True)
    seen_spread = predicted - seen_mean
    weighted = seen_spread * (1.0 / variance)[:, None, :]
    outer = jnp.einsum("pik,pjk->pij", weighted, seen_spread, precision=highest)
    scale = members - 1.0 + jnp.sqrt(jnp.sum(outer * outer, axis=(1, 2)))
    identity = jnp.eye(members, dtype=f32)
    current = ((members - 1.0) * identity + outer) / scale[:, None, None]
    root = jnp.broadcast_to(identity, current.shape)
    for sweep in range(SWEEPS):
        middle = 1.5 * identity - 0.5 * jnp.einsum("pij,pjk->pik", root, current, precision=highest)
        current = jnp.einsum("pij,pjk->pik", current, middle, precision=highest)
        root = jnp.einsum("pij,pjk->pik", middle, root, precision=highest)
    covariance = jnp.einsum("pij,pjk->pik", root, root, precision=highest) / scale[:, None, None]
    innovation = observed - seen_mean[:, 0, :]
    projected = jnp.einsum("pjk,pk->pj", weighted, innovation, precision=highest)
    coefficient = jnp.einsum("pij,pj->pi", covariance, projected, precision=highest)
    return jnp.sqrt((members - 1.0) / scale)[:, None, None] * root + coefficient[:, :, None]


def on_device(
    initial_concentrations,
    rate_field,
    kinetic_scaling_factors,
    observed_cell,
    measured_value,
    error_variance,
):
    group, tracers, band, longitudes = initial_concentrations.shape
    bands = lax.axis_size("grid")
    groups = lax.axis_size("mem")
    members = group * groups
    reactions = rate_field.shape[0]
    waves = NW // bands
    latitudes = band * bands
    own = band // groups
    patch_rows = own // PLAT
    cols = longitudes // PLON
    mem = lax.axis_index("mem")

    fourier = forward_transform(initial_concentrations, bands, waves)
    arrived = lax.all_to_all(fourier, "grid", split_axis=0, concat_axis=0, tiled=True)

    factors = lax.all_to_all(
        kinetic_scaling_factors.reshape(group, reactions, groups, patch_rows, cols).transpose(
            2, 0, 1, 3, 4
        ),
        "mem",
        split_axis=0,
        concat_axis=0,
        tiled=True,
    ).reshape(members, reactions, patch_rows, cols)
    ahead, back = meridional_tables(latitudes, own, bands, groups)
    gain = spectral_gain(latitudes, waves, bands)
    inverse = inverse_table(longitudes, waves, bands)
    rate = (
        lax.dynamic_slice_in_dim(rate_field, mem * own, own, 1)
        .astype(f32)
        .reshape(reactions, patch_rows, PLAT, longitudes)
        .transpose(0, 2, 1, 3)
    )
    factor = jnp.broadcast_to(
        factors.astype(f32).transpose(3, 0, 1, 2)[..., None],
        (cols, members, reactions, patch_rows, LANES),
    )

    def own_patches(array):
        mine = lax.dynamic_slice_in_dim(array, mem * patch_rows, patch_rows, 0)
        return mine.transpose(1, 0, 2)

    cell = own_patches(observed_cell)
    lane = cell % PLON
    place = cell // PLON
    observed = own_patches(measured_value)
    variance = own_patches(error_variance)

    last = meridional_transform(
        arrived.reshape(latitudes, group * tracers * 2 * waves),
        ahead,
        back,
        gain,
        waves,
        tracers,
        groups * bands,
    )
    returned = lax.all_to_all(last, ("mem", "grid"), split_axis=0, concat_axis=0, tiled=True)
    z = returned.reshape(groups, bands, group * tracers * own, 2 * waves)
    bg, seen = chemistry(z, inverse, rate, factor, lane, place, tracers)

    patches = cols * patch_rows
    predicted = seen.transpose(0, 2, 1, 3).reshape(patches, members, -1)
    transform = ensemble_transform(
        predicted, observed.reshape(patches, -1), variance.reshape(patches, -1)
    )
    weights = transform + (1.0 - jnp.sum(transform, axis=1, keepdims=True)) / members
    weights = weights.reshape(cols, patch_rows, members, members)
    same = jnp.eye(patch_rows, dtype=f32)
    spread = weights.transpose(0, 3, 1, 2)[..., None] * same[None, None, :, None, :]
    spread = spread.reshape(cols, members * patch_rows, members * patch_rows)
    high = spread.astype(bf16)
    low = (spread - high.astype(f32)).astype(bf16)
    analysed = apply_weights(high, low, bg, members, own)
    landed = lax.all_to_all(
        analysed.reshape(groups, group, tracers, own, longitudes),
        "mem",
        split_axis=0,
        concat_axis=0,
        tiled=True,
    )
    analysis = landed.transpose(1, 2, 0, 3, 4).reshape(group, tracers, band, longitudes)

    theta = jnp.log(factors.astype(f32)).transpose(3, 2, 0, 1).reshape(patches, members, reactions)
    theta_mean = jnp.mean(theta, axis=1, keepdims=True)
    theta_new = theta_mean + jnp.einsum(
        "pir,pij->pjr", theta - theta_mean, transform, precision=lax.Precision.HIGHEST
    )
    updated = (
        jnp.exp(theta_new)
        .astype(bf16)
        .reshape(cols, patch_rows, groups, group, reactions)
        .transpose(2, 3, 4, 1, 0)
    )
    updated = lax.all_to_all(updated, "mem", split_axis=0, concat_axis=0, tiled=True)
    mult_analysis = updated.transpose(1, 2, 0, 3, 4).reshape(
        group, reactions, groups * patch_rows, cols
    )
    return (analysis, mult_analysis)


def solution(mesh):
    return jax.shard_map(
        on_device,
        mesh=mesh,
        in_specs=(
            P("mem", None, "grid", None),
            P(None, "grid", None),
            P("mem", None, "grid", None),
            P("grid", None, None),
            P("grid", None, None),
            P("grid", None, None),
        ),
        out_specs=(P("mem", None, "grid", None), P("mem", None, "grid", None)),
        check_vma=False,
    )
```

```python
import functools
import math

import jax
import jax.numpy as jnp
from jax import lax
from jax.experimental import pallas as pl
from jax.experimental.pallas import tpu as pltpu
from jax.sharding import PartitionSpec as P

NW = 512
PLAT = 3
PLON = 256
SWEEPS = 5
LANES = 128
SUBLANES = 8
CHUNKS = 2


damping = 2.0
f32 = jnp.float32
bf16 = jnp.bfloat16


def rounded_angle(product, period):
    turns = jnp.floor(product * (1.0 / period))
    return (product - turns * period) * (2.0 * math.pi / period)


def forward_kernel(bands, waves, x_ref, o_ref, table, coarse, fine):
    tracers, band, longitudes = x_ref.shape[1:]
    columns = table.shape[1]
    local = 2 * waves
    step = fine.shape[1]

    @pl.when(pl.program_id(0) == 0)
    def _():
        def waves_of(rows):
            q = lax.broadcasted_iota(jnp.int32, (rows, columns), 1)
            p = q // local
            part = (q % local) // waves
            wave = bands * (q % waves) + p
            return wave.astype(f32), part

        rows = coarse.shape[1]
        wave, part = waves_of(rows)
        row = lax.broadcasted_iota(jnp.int32, (rows, columns), 0) * step
        angle = rounded_angle(wave * row.astype(f32), longitudes)
        cosine, sine = jnp.cos(angle), jnp.sin(angle)
        coarse[0] = jnp.where(part == 0, cosine, -sine)
        coarse[1] = jnp.where(part == 0, sine, cosine)
        wave, part = waves_of(step)
        row = lax.broadcasted_iota(jnp.int32, (step, columns), 0)
        angle = rounded_angle(wave * row.astype(f32), longitudes)
        fine[0] = jnp.cos(angle)
        fine[1] = jnp.sin(angle)

        def build(at, carry):
            block = coarse[0, pl.ds(at, 1), :] * fine[0] - coarse[1, pl.ds(at, 1), :] * fine[1]
            start = pl.multiple_of(at * step, step)
            table[pl.ds(start, step), :] = block.astype(bf16)
            return carry

        lax.fori_loop(0, rows, build, 0)

    x = x_ref[0].astype(bf16).reshape(tracers * band, longitudes)
    y = jnp.dot(x, table[...], preferred_element_type=f32) * (1.0 / longitudes)
    y = y.astype(bf16).reshape(tracers, band, columns)
    for t in range(tracers):
        for p in range(bands):
            o_ref[p, :, t * local : (t + 1) * local] = y[t, :, p * local : (p + 1) * local]


def forward_transform(x, bands, waves):
    group, tracers, band, longitudes = x.shape
    local = 2 * waves
    step = 32 if longitudes % 32 == 0 else 8
    return pl.pallas_call(
        functools.partial(forward_kernel, bands, waves),
        grid=(group,),
        in_specs=[pl.BlockSpec((1, tracers, band, longitudes), lambda g: (g, 0, 0, 0))],
        out_specs=pl.BlockSpec((bands, band, tracers * local), lambda g: (0, 0, g)),
        out_shape=jax.ShapeDtypeStruct((bands, band, group * tracers * local), bf16),
        scratch_shapes=[
            pltpu.VMEM((longitudes, bands * local), bf16),
            pltpu.VMEM((2, longitudes // step, bands * local), f32),
            pltpu.VMEM((2, step, bands * local), f32),
        ],
        compiler_params=pltpu.CompilerParams(vmem_limit_bytes=60 * 2**20),
        name="forward_dft",
    )(x)


def meridional_kernel(waves, a_ref, ahead_ref, back_ref, gain_ref, o_ref):
    local = 2 * waves
    tracers = a_ref.shape[1] // local
    spectrum = jnp.dot(ahead_ref[...], a_ref[...], preferred_element_type=f32)
    gain = jnp.concatenate([gain_ref[...]] * tracers, axis=1)
    damped = (spectrum * gain).astype(bf16)
    back = jnp.dot(back_ref[...], damped, preferred_element_type=f32).astype(bf16)
    owners, _, rows, _ = o_ref.shape
    own = rows // tracers
    for t in range(tracers):
        part = back[:, t * local : (t + 1) * local].reshape(owners, own, local)
        o_ref[:, 0, t * own : (t + 1) * own, :] = part


def meridional_transform(arrived, ahead, back, gain, waves, tracers, owners):
    latitudes, columns = arrived.shape
    local = 2 * waves
    group = columns // (tracers * local)
    own = latitudes // owners
    whole = lambda g: (0, 0)
    return pl.pallas_call(
        functools.partial(meridional_kernel, waves),
        grid=(group,),
        in_specs=[
            pl.BlockSpec((latitudes, tracers * local), lambda g: (0, g)),
            pl.BlockSpec(ahead.shape, whole),
            pl.BlockSpec(back.shape, whole),
            pl.BlockSpec(gain.shape, whole),
        ],
        out_specs=pl.BlockSpec((owners, 1, tracers * own, local), lambda g: (0, g, 0, 0)),
        out_shape=jax.ShapeDtypeStruct((owners, group, tracers * own, local), bf16),
        compiler_params=pltpu.CompilerParams(vmem_limit_bytes=60 * 2**20),
        name="meridional",
    )(arrived, ahead, back, gain)


def meridional_tables(latitudes, own, bands, groups):
    device = lax.axis_index("grid")
    even = device % 2 == 0
    modes = jnp.arange(NW, dtype=jnp.int32)
    order = jnp.where(even, modes, modes + 1).astype(f32)

    def values(theta, order):
        angle = theta * order
        return jnp.where(even, jnp.cos(angle), jnp.sin(angle)).astype(bf16)

    theta = (jnp.arange(latitudes, dtype=f32) + 0.5) * (math.pi / latitudes)
    ahead = values(theta[None, :], order[:, None])
    rows = own // PLAT
    index = (
        lax.broadcasted_iota(jnp.int32, (groups, bands, PLAT, rows), 0) * own
        + lax.broadcasted_iota(jnp.int32, (groups, bands, PLAT, rows), 1) * (own * groups)
        + lax.broadcasted_iota(jnp.int32, (groups, bands, PLAT, rows), 2)
        + lax.broadcasted_iota(jnp.int32, (groups, bands, PLAT, rows), 3) * PLAT
    ).reshape(latitudes)
    theta = (index.astype(f32) + 0.5) * (math.pi / latitudes)
    back = values(theta[:, None], order[None, :])
    return ahead, back


def spectral_gain(latitudes, waves, bands):
    device = lax.axis_index("grid")
    modes = jnp.arange(NW, dtype=jnp.int32)[:, None]
    column = jnp.arange(2 * waves, dtype=jnp.int32)[None, :]
    wave = bands * (column % waves) + device
    total = (wave + modes).astype(f32)
    ratio = total * (total + 1.0) / float(NW * (NW - 1))
    half = jnp.where((wave % 2 == 0) & (modes == 0), 0.5, 1.0)
    gain = half / (1.0 + damping * ratio * ratio)
    return jnp.where(wave + modes <= NW - 1, gain, 0.0) * (2.0 / latitudes)


def inverse_table(longitudes, waves, bands):
    q = jnp.arange(bands * 2 * waves, dtype=jnp.int32)
    device = q // (2 * waves)
    part = (q % (2 * waves)) // waves
    wave = bands * (q % waves) + device
    column = jnp.arange(longitudes, dtype=jnp.int32)
    phase = wave[:, None] * column[None, :] % longitudes
    phase = phase + jnp.where(part == 0, 0, longitudes // 4)[:, None]
    weight = jnp.where(wave == 0, 1.0, 2.0)[:, None]
    angle = phase.astype(f32) * (2.0 * math.pi / longitudes)
    return (weight * jnp.cos(angle)).astype(bf16)


def chemistry_kernel(
    z_ref, table_ref, rate_ref, factor_ref, lane_ref, place_ref, bg_ref, seen_ref, lhs, smooth, fresh
):
    sources, bands, rows, local = z_ref.shape
    reactions, height, patch_rows, _ = rate_ref.shape
    members = factor_ref.shape[1]
    tracers = bg_ref.shape[0]
    others = tracers - 1

    @pl.when(pl.program_id(0) == 0)
    def _():
        for s in range(sources):
            for p in range(bands):
                lhs[s * rows : (s + 1) * rows, p * local : (p + 1) * local] = z_ref[s, p]

    smooth[...] = jnp.dot(lhs[...], table_ref[...], preferred_element_type=f32).reshape(
        members, tracers, height, patch_rows, PLON
    )

    def one_member(e, carry):
        for i in range(height):
            for at in range(0, PLON, LANES):
                lanes = slice(at, at + LANES)
                rates = [
                    factor_ref[0, e, r] * rate_ref[r, i, :, lanes] for r in range(reactions)
                ]
                kept = []
                for a in range(tracers):
                    outflow = rates[others * a]
                    for s in range(1, others):
                        outflow = outflow + rates[others * a + s]
                    kept.append(smooth[e, a, i, :, lanes] * (1.0 / (1.0 + outflow)))
                for b in range(tracers):
                    value = kept[b]
                    for a in range(tracers):
                        if a != b:
                            s = b if b < a else b - 1
                            value = value + rates[others * a + s] * kept[a]
                    fresh[b, i, e, :, lanes] = value
        return carry

    lax.fori_loop(0, members, one_member, 0)
    for t in range(tracers):
        for i in range(height):
            bg_ref[t, i] = fresh[t, i].reshape(members * patch_rows, PLON).astype(bf16)

    copies = max(1, SUBLANES // patch_rows)

    def tiled(array):
        return jnp.concatenate([array] * copies, axis=0) if copies > 1 else array

    lane = tiled(lane_ref[0])
    place = tiled(place_ref[0])
    within = lane % LANES
    piece = lane // LANES

    def observe(e, carry):
        seen = jnp.zeros(lane.shape, f32)
        for t in range(tracers):
            for i in range(height):
                value = tiled(fresh[t, i, e])
                for k in range(PLON // LANES):
                    found = jnp.take_along_axis(
                        value[:, k * LANES : (k + 1) * LANES],
                        within,
                        axis=1,
                        mode="promise_in_bounds",
                    )
                    here = (place == t * height + i) & (piece == k)
                    seen = jnp.where(here, found, seen)
        seen_ref[0, e] = seen[:patch_rows].astype(bf16).astype(f32)
        return carry

    lax.fori_loop(0, members, observe, 0)


def chemistry(z, table, rate, factor, lane, place, tracers, base, cols):
    sources, bands, rows, local = z.shape
    reactions, height, patch_rows, _ = rate.shape
    members = factor.shape[1]
    observations = lane.shape[-1]
    return pl.pallas_call(
        chemistry_kernel,
        grid=(cols,),
        in_specs=[
            pl.BlockSpec(z.shape, lambda c: (0, 0, 0, 0)),
            pl.BlockSpec((table.shape[0], PLON), lambda c: (0, c + base)),
            pl.BlockSpec((reactions, height, patch_rows, PLON), lambda c: (0, 0, 0, c + base)),
            pl.BlockSpec((1, members, reactions, patch_rows, LANES), lambda c: (c + base, 0, 0, 0, 0)),
            pl.BlockSpec((1, patch_rows, observations), lambda c: (c + base, 0, 0)),
            pl.BlockSpec((1, patch_rows, observations), lambda c: (c + base, 0, 0)),
        ],
        out_specs=[
            pl.BlockSpec((tracers, height, members * patch_rows, PLON), lambda c: (0, 0, 0, c)),
            pl.BlockSpec((1, members, patch_rows, observations), lambda c: (c, 0, 0, 0)),
        ],
        out_shape=[
            jax.ShapeDtypeStruct((tracers, height, members * patch_rows, cols * PLON), bf16),
            jax.ShapeDtypeStruct((cols, members, patch_rows, observations), f32),
        ],
        scratch_shapes=[
            pltpu.VMEM((sources * rows, bands * local), bf16),
            pltpu.VMEM((members, tracers, height, patch_rows, PLON), f32),
            pltpu.VMEM((tracers, height, members, patch_rows, PLON), f32),
        ],
        compiler_params=pltpu.CompilerParams(vmem_limit_bytes=60 * 2**20),
        cost_estimate=pl.CostEstimate(
            flops=2 * sources * rows * bands * local * cols * PLON,
            bytes_accessed=2 * math.prod(z.shape) * 8,
            transcendentals=0,
        ),
        name="chemistry",
    )(z, table, rate, factor, lane, place)


def precise_dot(a, b):
    return jnp.dot(a, b, preferred_element_type=f32, precision=lax.Precision.HIGHEST)


def member_weights(seen, measured, variance, members, patch_rows):
    wide = members * patch_rows
    row = lax.broadcasted_iota(jnp.int32, (wide, wide), 0)
    column = lax.broadcasted_iota(jnp.int32, (wide, wide), 1)
    mask = (row % patch_rows == column % patch_rows).astype(f32)
    identity = (row == column).astype(f32)
    spare = members - 1.0

    def over_members(array):
        return jnp.sum(array.reshape(members, patch_rows, array.shape[-1]), axis=0)

    def each_member(array):
        return jnp.concatenate([array] * members, axis=0)

    currents, scales, projections = [], [], []
    for predicted, observed, errors in zip(seen, measured, variance):
        mean = over_members(predicted) * (1.0 / members)
        spread = predicted - each_member(mean)
        weighted = spread * each_member(1.0 / errors)
        outer = mask * lax.dot_general(
            weighted,
            spread,
            (((1,), (1,)), ((), ())),
            preferred_element_type=f32,
            precision=lax.Precision.HIGHEST,
        )
        square = over_members(jnp.sum(outer * outer, axis=1, keepdims=True))
        scale = each_member(spare + jnp.sqrt(square))
        currents.append((spare * identity + outer) * (1.0 / scale))
        scales.append(scale)
        innovation = each_member(observed - mean)
        projections.append(jnp.sum(weighted * innovation, axis=1, keepdims=True))

    roots = [1.5 * identity - 0.5 * current for current in currents]
    currents = [precise_dot(c, m) for c, m in zip(currents, roots)]
    for sweep in range(1, SWEEPS):
        middles = [
            1.5 * identity - 0.5 * precise_dot(r, c) for r, c in zip(roots, currents)
        ]
        if sweep < SWEEPS - 1:
            currents = [precise_dot(c, m) for c, m in zip(currents, middles)]
        roots = [precise_dot(m, r) for m, r in zip(middles, roots)]

    weights = []
    for root, scale, projected in zip(roots, scales, projections):
        along = jnp.sum(identity * projected, axis=0, keepdims=True)
        once = jnp.sum(root * along, axis=1, keepdims=True)
        twice = jnp.sum(root * (once * (1.0 / scale)), axis=0, keepdims=True)
        transform = jnp.sqrt(spare / scale) * root + mask * twice
        rest = (1.0 - jnp.sum(transform, axis=1, keepdims=True)) * (1.0 / members)
        weights.append(transform + mask * rest)
    return weights


def analysis_kernel(groups, me_ref, seen_ref, measured_ref, variance_ref, theta_ref, bg_ref, *refs):
    outs, factors = refs[:groups], refs[groups : 2 * groups]
    high, low, rows = refs[2 * groups :]
    cols, patch_rows, _ = measured_ref.shape
    group, tracers, own, _ = outs[0].shape
    members = groups * group
    height = own // patch_rows
    block = group * patch_rows
    at = pl.program_id(0)

    @pl.when(at == 0)
    def _():
        weights = member_weights(
            [seen_ref[c] for c in range(cols)],
            [measured_ref[c] for c in range(cols)],
            [variance_ref[c] for c in range(cols)],
            members,
            patch_rows,
        )
        for c in range(cols):
            upper = weights[c].astype(bf16)
            high[c] = weights[c]
            low[c] = weights[c] - upper.astype(f32)

    def by_partner(ref):
        parts = []
        for j in range(groups):
            start = pl.multiple_of((me_ref[0] ^ j) * block, block)
            parts.append(ref[at, pl.ds(start, block), :])
        return jnp.concatenate(parts, axis=0)

    exact = by_partner(high)
    updated = jnp.exp(precise_dot(exact, theta_ref[0])).astype(bf16)
    for j in range(groups):
        factors[j][0] = updated[j * block : (j + 1) * block]
    upper = exact.astype(bf16)
    lower = by_partner(low).astype(bf16)
    for t in range(tracers):
        for i in range(height):
            value = bg_ref[t, i]
            new = jnp.dot(upper, value, preferred_element_type=f32)
            new = new + jnp.dot(lower, value, preferred_element_type=f32)
            for e in range(members):
                part = new[e * patch_rows : (e + 1) * patch_rows]
                for k in range(PLON // LANES):
                    rows[k, e, pl.ds(i, patch_rows, stride=height), :] = part[
                        :, k * LANES : (k + 1) * LANES
                    ]
        for j in range(groups):
            for k in range(PLON // LANES):
                outs[j][:, t, :, k * LANES : (k + 1) * LANES] = rows[
                    k, j * group : (j + 1) * group
                ].astype(bf16)


def analyse(me, seen, measured, variance, theta, bg, base, groups, own):
    cols, members, patch_rows, observations = seen.shape
    group = members // groups
    tracers, height, wide, longitudes = bg.shape
    block = group * patch_rows
    lanes = theta.shape[-1]
    whole = lambda c, me: (0, 0, 0)
    shifted = lambda c, me: (base // cols, 0, 0)
    return pl.pallas_call(
        functools.partial(analysis_kernel, groups),
        grid_spec=pltpu.PrefetchScalarGridSpec(
            num_scalar_prefetch=1,
            grid=(cols,),
            in_specs=[
                pl.BlockSpec((cols, wide, observations), whole),
                pl.BlockSpec((cols, patch_rows, observations), shifted),
                pl.BlockSpec((cols, patch_rows, observations), shifted),
                pl.BlockSpec((1, wide, lanes), lambda c, me: (c + base, 0, 0)),
                pl.BlockSpec((tracers, height, wide, PLON), lambda c, me: (0, 0, 0, c)),
            ],
            out_specs=[pl.BlockSpec((group, tracers, own, PLON), lambda c, me: (0, 0, 0, c))]
            * groups
            + [pl.BlockSpec((1, block, lanes), lambda c, me: (c, 0, 0))] * groups,
            scratch_shapes=[
                pltpu.VMEM((cols, wide, wide), f32),
                pltpu.VMEM((cols, wide, wide), f32),
                pltpu.VMEM((PLON // LANES, members, own, LANES), f32),
            ],
        ),
        out_shape=[jax.ShapeDtypeStruct((group, tracers, own, longitudes), bf16)] * groups
        + [jax.ShapeDtypeStruct((cols, block, lanes), bf16)] * groups,
        compiler_params=pltpu.CompilerParams(vmem_limit_bytes=60 * 2**20),
        cost_estimate=pl.CostEstimate(
            flops=6 * 10**9, bytes_accessed=8 * tracers * height * wide * longitudes, transcendentals=0
        ),
        name="analysis",
    )(me, seen.reshape(cols, wide, observations), measured, variance, theta, bg)


def assemble_kernel(groups, first, lanes, me_ref, *refs):
    pieces = refs[:groups]
    out = refs[groups + (0 if first else 1)]
    buffer, arrived, left = refs[-3:]
    own = pieces[0].shape[2]
    ins, outs = [], []
    for j in range(groups):
        ins.append(pltpu.make_async_copy(pieces[j], buffer.at[j], arrived.at[j]))
        ins[j].start()
    for j in range(groups):
        start = pl.multiple_of((me_ref[0] ^ j) * own, own)
        ins[j].wait()
        outs.append(
            pltpu.make_async_copy(
                buffer.at[j], out.at[:, :, pl.ds(start, own), lanes], left.at[j]
            )
        )
        outs[j].start()
    for j in range(groups):
        outs[j].wait()


def assemble(me, pieces, before, start, shape):
    groups = len(pieces)
    width = pieces[0].shape[-1]
    any_spec = pl.BlockSpec(memory_space=pl.ANY)
    extra = [] if before is None else [before]
    return pl.pallas_call(
        functools.partial(assemble_kernel, groups, before is None, pl.ds(start, width)),
        grid_spec=pltpu.PrefetchScalarGridSpec(
            num_scalar_prefetch=1,
            grid=(1,),
            in_specs=[any_spec] * (groups + len(extra)),
            out_specs=any_spec,
            scratch_shapes=[
                pltpu.VMEM((groups,) + pieces[0].shape, bf16),
                pltpu.SemaphoreType.DMA((groups,)),
                pltpu.SemaphoreType.DMA((groups,)),
            ],
        ),
        out_shape=jax.ShapeDtypeStruct(shape, bf16),
        input_output_aliases={} if before is None else {groups + 1: 0},
        compiler_params=pltpu.CompilerParams(vmem_limit_bytes=40 * 2**20),
        cost_estimate=pl.CostEstimate(
            flops=0, bytes_accessed=2 * 2 * groups * math.prod(pieces[0].shape), transcendentals=0
        ),
        name="assemble",
    )(me, *pieces, *extra)


def on_device(
    initial_concentrations,
    rate_field,
    kinetic_scaling_factors,
    observed_cell,
    measured_value,
    error_variance,
):
    group, tracers, band, longitudes = initial_concentrations.shape
    bands = lax.axis_size("grid")
    groups = lax.axis_size("mem")
    members = group * groups
    reactions = rate_field.shape[0]
    waves = NW // bands
    latitudes = band * bands
    own = band // groups
    patch_rows = own // PLAT
    cols = longitudes // PLON
    mem = lax.axis_index("mem")

    fourier = forward_transform(initial_concentrations, bands, waves)
    arrived = lax.all_to_all(fourier, "grid", split_axis=0, concat_axis=0, tiled=True)

    factors = lax.all_to_all(
        kinetic_scaling_factors.reshape(group, reactions, groups, patch_rows, cols).transpose(
            2, 0, 1, 3, 4
        ),
        "mem",
        split_axis=0,
        concat_axis=0,
        tiled=True,
    ).reshape(members, reactions, patch_rows, cols)
    ahead, back = meridional_tables(latitudes, own, bands, groups)
    gain = spectral_gain(latitudes, waves, bands)
    inverse = inverse_table(longitudes, waves, bands)
    rate = (
        lax.dynamic_slice_in_dim(rate_field, mem * own, own, 1)
        .astype(f32)
        .reshape(reactions, patch_rows, PLAT, longitudes)
        .transpose(0, 2, 1, 3)
    )
    factor = jnp.broadcast_to(
        factors.astype(f32).transpose(3, 0, 1, 2)[..., None],
        (cols, members, reactions, patch_rows, LANES),
    )

    def own_patches(array):
        mine = lax.dynamic_slice_in_dim(array, mem * patch_rows, patch_rows, 0)
        return mine.transpose(1, 0, 2)

    cell = own_patches(observed_cell)
    lane = cell % PLON
    place = cell // PLON
    observed = own_patches(measured_value)
    variance = own_patches(error_variance)

    last = meridional_transform(
        arrived.reshape(latitudes, group * tracers * 2 * waves),
        ahead,
        back,
        gain,
        waves,
        tracers,
        groups * bands,
    )
    returned = lax.all_to_all(last, ("mem", "grid"), split_axis=0, concat_axis=0, tiled=True)
    z = returned.reshape(groups, bands, group * tracers * own, 2 * waves)
    me = mem.astype(jnp.int32).reshape(1)
    theta = jnp.pad(
        jnp.log(factors.astype(f32)).transpose(3, 0, 2, 1),
        ((0, 0), (0, 0), (0, 0), (0, LANES - reactions)),
    ).reshape(cols, members * patch_rows, LANES)

    chunks = CHUNKS if cols % CHUNKS == 0 else 1
    per = cols // chunks
    landed, updated = [], []
    for chunk in range(chunks):
        base = chunk * per
        bg, seen = chemistry(z, inverse, rate, factor, lane, place, tracers, base, per)
        results = analyse(me, seen, observed, variance, theta, bg, base, groups, own)
        if chunk < chunks - 1:
            z, results = lax.optimization_barrier((z, results))
        sent = []
        for j, result in enumerate(results):
            pairs = [(i, i ^ (j % groups)) for i in range(groups)]
            sent.append(result if j % groups == 0 else lax.ppermute(result, "mem", pairs))
        landed.append(sent[:groups])
        updated.append(sent[groups:])

    shape = (group, tracers, band, longitudes)
    order = mem ^ jnp.arange(groups, dtype=jnp.int32)
    if own % SUBLANES == 0:
        analysis = None
        for chunk in range(chunks):
            analysis = assemble(me, landed[chunk], analysis, chunk * per * PLON, shape)
    else:
        joined = jnp.stack(
            [jnp.concatenate([part[j] for part in landed], axis=-1) for j in range(groups)]
        )
        joined = jnp.take(joined, order, axis=0)
        analysis = joined.transpose(1, 2, 0, 3, 4).reshape(shape)
    fresh = jnp.stack([jnp.concatenate([part[j] for part in updated]) for j in range(groups)])
    fresh = fresh[..., :reactions].reshape(groups, cols, group, patch_rows, reactions)
    mine = (order[:, None] == jnp.arange(groups, dtype=jnp.int32)[None, :]).astype(bf16)
    mult_analysis = jnp.einsum(
        "jr,jcgpa->garpc", mine, fresh, preferred_element_type=f32
    ).astype(bf16)
    mult_analysis = mult_analysis.reshape(group, reactions, groups * patch_rows, cols)
    return (analysis, mult_analysis)


def solution(mesh):
    return jax.shard_map(
        on_device,
        mesh=mesh,
        in_specs=(
            P("mem", None, "grid", None),
            P(None, "grid", None),
            P("mem", None, "grid", None),
            P("grid", None, None),
            P("grid", None, None),
            P("grid", None, None),
        ),
        out_specs=(P("mem", None, "grid", None), P("mem", None, "grid", None)),
        check_vma=False,
    )
```

```python
import functools
import math

import jax
import jax.numpy as jnp
from jax import lax
from jax.experimental import pallas as pl
from jax.experimental.pallas import tpu as pltpu
from jax.sharding import PartitionSpec as P

NW = 512
PLAT = 3
PLON = 256
SWEEPS = 5
LANES = 128
SUBLANES = 8
CHUNKS = 2


damping = 2.0
f32 = jnp.float32
bf16 = jnp.bfloat16


def rounded_angle(product, period):
    turns = jnp.floor(product * (1.0 / period))
    return (product - turns * period) * (2.0 * math.pi / period)


def forward_kernel(bands, waves, me_ref, x_ref, *refs):
    outs = refs[:bands]
    table, coarse, fine = refs[bands:]
    tracers, band, longitudes = x_ref.shape[1:]
    columns = table.shape[1]
    local = 2 * waves
    step = fine.shape[1]

    @pl.when(pl.program_id(0) == 0)
    def _():
        def waves_of(rows):
            q = lax.broadcasted_iota(jnp.int32, (rows, columns), 1)
            p = (q // local) ^ me_ref[0]
            part = (q % local) // waves
            wave = bands * (q % waves) + p
            return wave.astype(f32), part

        rows = coarse.shape[1]
        wave, part = waves_of(rows)
        row = lax.broadcasted_iota(jnp.int32, (rows, columns), 0) * step
        angle = rounded_angle(wave * row.astype(f32), longitudes)
        cosine, sine = jnp.cos(angle), jnp.sin(angle)
        coarse[0] = jnp.where(part == 0, cosine, -sine)
        coarse[1] = jnp.where(part == 0, sine, cosine)
        wave, part = waves_of(step)
        row = lax.broadcasted_iota(jnp.int32, (step, columns), 0)
        angle = rounded_angle(wave * row.astype(f32), longitudes)
        fine[0] = jnp.cos(angle)
        fine[1] = jnp.sin(angle)

        def build(at, carry):
            block = coarse[0, pl.ds(at, 1), :] * fine[0] - coarse[1, pl.ds(at, 1), :] * fine[1]
            start = pl.multiple_of(at * step, step)
            table[pl.ds(start, step), :] = block.astype(bf16)
            return carry

        lax.fori_loop(0, rows, build, 0)

    x = x_ref[0].astype(bf16).reshape(tracers * band, longitudes)
    y = jnp.dot(x, table[...], preferred_element_type=f32) * (1.0 / longitudes)
    y = y.astype(bf16).reshape(tracers, band, columns)
    for t in range(tracers):
        for k in range(bands):
            outs[k][:, t * local : (t + 1) * local] = y[t, :, k * local : (k + 1) * local]


def forward_transform(me, x, bands, waves):
    group, tracers, band, longitudes = x.shape
    local = 2 * waves
    step = 32 if longitudes % 32 == 0 else 8
    return pl.pallas_call(
        functools.partial(forward_kernel, bands, waves),
        grid_spec=pltpu.PrefetchScalarGridSpec(
            num_scalar_prefetch=1,
            grid=(group,),
            in_specs=[pl.BlockSpec((1, tracers, band, longitudes), lambda g, me: (g, 0, 0, 0))],
            out_specs=[pl.BlockSpec((band, tracers * local), lambda g, me: (0, g))] * bands,
            scratch_shapes=[
                pltpu.VMEM((longitudes, bands * local), bf16),
                pltpu.VMEM((2, longitudes // step, bands * local), f32),
                pltpu.VMEM((2, step, bands * local), f32),
            ],
        ),
        out_shape=[jax.ShapeDtypeStruct((band, group * tracers * local), bf16)] * bands,
        compiler_params=pltpu.CompilerParams(vmem_limit_bytes=60 * 2**20),
        name="forward_dft",
    )(me, x)


def meridional_kernel(waves, bands, *refs):
    pieces = refs[:bands]
    ahead_ref, back_ref, gain_ref, o_ref, arrived = refs[bands:]
    local = 2 * waves
    band, columns = pieces[0].shape
    tracers = columns // local
    for k in range(bands):
        arrived[k * band : (k + 1) * band, :] = pieces[k][...]
    spectrum = jnp.dot(ahead_ref[...], arrived[...], preferred_element_type=f32)
    gain = jnp.concatenate([gain_ref[...]] * tracers, axis=1)
    damped = (spectrum * gain).astype(bf16)
    back = jnp.dot(back_ref[...], damped, preferred_element_type=f32).astype(bf16)
    owners, _, rows, _ = o_ref.shape
    own = rows // tracers
    for t in range(tracers):
        part = back[:, t * local : (t + 1) * local].reshape(owners, own, local)
        o_ref[:, 0, t * own : (t + 1) * own, :] = part


def meridional_transform(arrived, ahead, back, gain, waves, tracers, owners):
    band, columns = arrived[0].shape
    bands = len(arrived)
    latitudes = bands * band
    local = 2 * waves
    group = columns // (tracers * local)
    own = latitudes // owners
    whole = lambda g: (0, 0)
    return pl.pallas_call(
        functools.partial(meridional_kernel, waves, bands),
        grid=(group,),
        in_specs=[pl.BlockSpec((band, tracers * local), lambda g: (0, g))] * bands
        + [
            pl.BlockSpec(ahead.shape, whole),
            pl.BlockSpec(back.shape, whole),
            pl.BlockSpec(gain.shape, whole),
        ],
        out_specs=pl.BlockSpec((owners, 1, tracers * own, local), lambda g: (0, g, 0, 0)),
        out_shape=jax.ShapeDtypeStruct((owners, group, tracers * own, local), bf16),
        compiler_params=pltpu.CompilerParams(vmem_limit_bytes=60 * 2**20),
        scratch_shapes=[pltpu.VMEM((latitudes, tracers * local), bf16)],
        cost_estimate=pl.CostEstimate(
            flops=4 * latitudes * NW * columns,
            bytes_accessed=4 * latitudes * columns,
            transcendentals=0,
        ),
        name="meridional",
    )(*arrived, ahead, back, gain)


def meridional_tables(latitudes, own, bands, groups):
    device = lax.axis_index("grid")
    even = device % 2 == 0
    modes = jnp.arange(NW, dtype=jnp.int32)
    order = jnp.where(even, modes, modes + 1).astype(f32)

    def values(theta, order):
        angle = theta * order
        return jnp.where(even, jnp.cos(angle), jnp.sin(angle)).astype(bf16)

    band = own * groups
    lat = jnp.arange(latitudes, dtype=jnp.int32)
    lat = ((lat // band) ^ device) * band + lat % band
    theta = (lat.astype(f32) + 0.5) * (math.pi / latitudes)
    ahead = values(theta[None, :], order[:, None])
    rows = own // PLAT
    index = (
        lax.broadcasted_iota(jnp.int32, (groups, bands, PLAT, rows), 0) * own
        + lax.broadcasted_iota(jnp.int32, (groups, bands, PLAT, rows), 1) * (own * groups)
        + lax.broadcasted_iota(jnp.int32, (groups, bands, PLAT, rows), 2)
        + lax.broadcasted_iota(jnp.int32, (groups, bands, PLAT, rows), 3) * PLAT
    ).reshape(latitudes)
    theta = (index.astype(f32) + 0.5) * (math.pi / latitudes)
    back = values(theta[:, None], order[None, :])
    return ahead, back


def spectral_gain(latitudes, waves, bands):
    device = lax.axis_index("grid")
    modes = jnp.arange(NW, dtype=jnp.int32)[:, None]
    column = jnp.arange(2 * waves, dtype=jnp.int32)[None, :]
    wave = bands * (column % waves) + device
    total = (wave + modes).astype(f32)
    ratio = total * (total + 1.0) / float(NW * (NW - 1))
    half = jnp.where((wave % 2 == 0) & (modes == 0), 0.5, 1.0)
    gain = half / (1.0 + damping * ratio * ratio)
    return jnp.where(wave + modes <= NW - 1, gain, 0.0) * (2.0 / latitudes)


def inverse_table(longitudes, waves, bands):
    q = jnp.arange(bands * 2 * waves, dtype=jnp.int32)
    device = q // (2 * waves)
    part = (q % (2 * waves)) // waves
    wave = bands * (q % waves) + device
    column = jnp.arange(longitudes, dtype=jnp.int32)
    phase = wave[:, None] * column[None, :] % longitudes
    phase = phase + jnp.where(part == 0, 0, longitudes // 4)[:, None]
    weight = jnp.where(wave == 0, 1.0, 2.0)[:, None]
    angle = phase.astype(f32) * (2.0 * math.pi / longitudes)
    return (weight * jnp.cos(angle)).astype(bf16)


def chemistry_kernel(
    z_ref, table_ref, rate_ref, factor_ref, lane_ref, place_ref, bg_ref, seen_ref, lhs, smooth, fresh
):
    sources, bands, rows, local = z_ref.shape
    reactions, height, patch_rows, _ = rate_ref.shape
    members = factor_ref.shape[1]
    tracers = bg_ref.shape[0]
    others = tracers - 1

    @pl.when(pl.program_id(0) == 0)
    def _():
        for s in range(sources):
            for p in range(bands):
                lhs[s * rows : (s + 1) * rows, p * local : (p + 1) * local] = z_ref[s, p]

    smooth[...] = jnp.dot(lhs[...], table_ref[...], preferred_element_type=f32).reshape(
        members, tracers, height, patch_rows, PLON
    )

    def one_member(e, carry):
        for i in range(height):
            for at in range(0, PLON, LANES):
                lanes = slice(at, at + LANES)
                rates = [
                    factor_ref[0, e, r] * rate_ref[r, i, :, lanes] for r in range(reactions)
                ]
                kept = []
                for a in range(tracers):
                    outflow = rates[others * a]
                    for s in range(1, others):
                        outflow = outflow + rates[others * a + s]
                    kept.append(smooth[e, a, i, :, lanes] * (1.0 / (1.0 + outflow)))
                for b in range(tracers):
                    value = kept[b]
                    for a in range(tracers):
                        if a != b:
                            s = b if b < a else b - 1
                            value = value + rates[others * a + s] * kept[a]
                    fresh[b, i, e, :, lanes] = value
        return carry

    lax.fori_loop(0, members, one_member, 0)
    for t in range(tracers):
        for i in range(height):
            bg_ref[t, i] = fresh[t, i].reshape(members * patch_rows, PLON).astype(bf16)

    copies = max(1, SUBLANES // patch_rows)

    def tiled(array):
        return jnp.concatenate([array] * copies, axis=0) if copies > 1 else array

    lane = tiled(lane_ref[0])
    place = tiled(place_ref[0])
    within = lane % LANES
    piece = lane // LANES

    def observe(e, carry):
        seen = jnp.zeros(lane.shape, f32)
        for t in range(tracers):
            for i in range(height):
                value = tiled(fresh[t, i, e])
                for k in range(PLON // LANES):
                    found = jnp.take_along_axis(
                        value[:, k * LANES : (k + 1) * LANES],
                        within,
                        axis=1,
                        mode="promise_in_bounds",
                    )
                    here = (place == t * height + i) & (piece == k)
                    seen = jnp.where(here, found, seen)
        seen_ref[0, e] = seen[:patch_rows].astype(bf16).astype(f32)
        return carry

    lax.fori_loop(0, members, observe, 0)


def chemistry(z, table, rate, factor, lane, place, tracers, base, cols):
    sources, bands, rows, local = z.shape
    reactions, height, patch_rows, _ = rate.shape
    members = factor.shape[1]
    observations = lane.shape[-1]
    return pl.pallas_call(
        chemistry_kernel,
        grid=(cols,),
        in_specs=[
            pl.BlockSpec(z.shape, lambda c: (0, 0, 0, 0)),
            pl.BlockSpec((table.shape[0], PLON), lambda c: (0, c + base)),
            pl.BlockSpec((reactions, height, patch_rows, PLON), lambda c: (0, 0, 0, c + base)),
            pl.BlockSpec((1, members, reactions, patch_rows, LANES), lambda c: (c + base, 0, 0, 0, 0)),
            pl.BlockSpec((1, patch_rows, observations), lambda c: (c + base, 0, 0)),
            pl.BlockSpec((1, patch_rows, observations), lambda c: (c + base, 0, 0)),
        ],
        out_specs=[
            pl.BlockSpec((tracers, height, members * patch_rows, PLON), lambda c: (0, 0, 0, c)),
            pl.BlockSpec((1, members, patch_rows, observations), lambda c: (c, 0, 0, 0)),
        ],
        out_shape=[
            jax.ShapeDtypeStruct((tracers, height, members * patch_rows, cols * PLON), bf16),
            jax.ShapeDtypeStruct((cols, members, patch_rows, observations), f32),
        ],
        scratch_shapes=[
            pltpu.VMEM((sources * rows, bands * local), bf16),
            pltpu.VMEM((members, tracers, height, patch_rows, PLON), f32),
            pltpu.VMEM((tracers, height, members, patch_rows, PLON), f32),
        ],
        compiler_params=pltpu.CompilerParams(vmem_limit_bytes=60 * 2**20),
        cost_estimate=pl.CostEstimate(
            flops=2 * sources * rows * bands * local * cols * PLON,
            bytes_accessed=2 * math.prod(z.shape) * 8,
            transcendentals=0,
        ),
        name="chemistry",
    )(z, table, rate, factor, lane, place)


def precise_dot(a, b):
    return jnp.dot(a, b, preferred_element_type=f32, precision=lax.Precision.HIGHEST)


def member_weights(seen, measured, variance, members, patch_rows):
    wide = members * patch_rows
    row = lax.broadcasted_iota(jnp.int32, (wide, wide), 0)
    column = lax.broadcasted_iota(jnp.int32, (wide, wide), 1)
    mask = (row % patch_rows == column % patch_rows).astype(f32)
    identity = (row == column).astype(f32)
    spare = members - 1.0

    def over_members(array):
        return jnp.sum(array.reshape(members, patch_rows, array.shape[-1]), axis=0)

    def each_member(array):
        return jnp.concatenate([array] * members, axis=0)

    currents, scales, projections = [], [], []
    for predicted, observed, errors in zip(seen, measured, variance):
        mean = over_members(predicted) * (1.0 / members)
        spread = predicted - each_member(mean)
        weighted = spread * each_member(1.0 / errors)
        outer = mask * lax.dot_general(
            weighted,
            spread,
            (((1,), (1,)), ((), ())),
            preferred_element_type=f32,
            precision=lax.Precision.HIGHEST,
        )
        square = over_members(jnp.sum(outer * outer, axis=1, keepdims=True))
        scale = each_member(spare + jnp.sqrt(square))
        currents.append((spare * identity + outer) * (1.0 / scale))
        scales.append(scale)
        innovation = each_member(observed - mean)
        projections.append(jnp.sum(weighted * innovation, axis=1, keepdims=True))

    roots = [1.5 * identity - 0.5 * current for current in currents]
    currents = [precise_dot(c, m) for c, m in zip(currents, roots)]
    for sweep in range(1, SWEEPS):
        middles = [
            1.5 * identity - 0.5 * precise_dot(r, c) for r, c in zip(roots, currents)
        ]
        if sweep < SWEEPS - 1:
            currents = [precise_dot(c, m) for c, m in zip(currents, middles)]
        roots = [precise_dot(m, r) for m, r in zip(middles, roots)]

    weights = []
    for root, scale, projected in zip(roots, scales, projections):
        along = jnp.sum(identity * projected, axis=0, keepdims=True)
        once = jnp.sum(root * along, axis=1, keepdims=True)
        twice = jnp.sum(root * (once * (1.0 / scale)), axis=0, keepdims=True)
        transform = jnp.sqrt(spare / scale) * root + mask * twice
        rest = (1.0 - jnp.sum(transform, axis=1, keepdims=True)) * (1.0 / members)
        weights.append(transform + mask * rest)
    return weights


def analysis_kernel(groups, me_ref, seen_ref, measured_ref, variance_ref, theta_ref, bg_ref, *refs):
    outs, factors = refs[:groups], refs[groups : 2 * groups]
    high, low, rows = refs[2 * groups :]
    cols, patch_rows, _ = measured_ref.shape
    group, tracers, own, _ = outs[0].shape
    members = groups * group
    height = own // patch_rows
    block = group * patch_rows
    at = pl.program_id(0)

    @pl.when(at == 0)
    def _():
        weights = member_weights(
            [seen_ref[c] for c in range(cols)],
            [measured_ref[c] for c in range(cols)],
            [variance_ref[c] for c in range(cols)],
            members,
            patch_rows,
        )
        for c in range(cols):
            upper = weights[c].astype(bf16)
            high[c] = weights[c]
            low[c] = weights[c] - upper.astype(f32)

    def by_partner(ref):
        parts = []
        for j in range(groups):
            start = pl.multiple_of((me_ref[0] ^ j) * block, block)
            parts.append(ref[at, pl.ds(start, block), :])
        return jnp.concatenate(parts, axis=0)

    exact = by_partner(high)
    updated = jnp.exp(precise_dot(exact, theta_ref[0])).astype(bf16)
    for j in range(groups):
        factors[j][0] = updated[j * block : (j + 1) * block]
    upper = exact.astype(bf16)
    lower = by_partner(low).astype(bf16)
    for t in range(tracers):
        for i in range(height):
            value = bg_ref[t, i]
            new = jnp.dot(upper, value, preferred_element_type=f32)
            new = new + jnp.dot(lower, value, preferred_element_type=f32)
            for e in range(members):
                part = new[e * patch_rows : (e + 1) * patch_rows]
                for k in range(PLON // LANES):
                    rows[k, e, pl.ds(i, patch_rows, stride=height), :] = part[
                        :, k * LANES : (k + 1) * LANES
                    ]
        for j in range(groups):
            for k in range(PLON // LANES):
                outs[j][:, t, :, k * LANES : (k + 1) * LANES] = rows[
                    k, j * group : (j + 1) * group
                ].astype(bf16)


def analyse(me, seen, measured, variance, theta, bg, base, groups, own):
    cols, members, patch_rows, observations = seen.shape
    group = members // groups
    tracers, height, wide, longitudes = bg.shape
    block = group * patch_rows
    lanes = theta.shape[-1]
    whole = lambda c, me: (0, 0, 0)
    shifted = lambda c, me: (base // cols, 0, 0)
    return pl.pallas_call(
        functools.partial(analysis_kernel, groups),
        grid_spec=pltpu.PrefetchScalarGridSpec(
            num_scalar_prefetch=1,
            grid=(cols,),
            in_specs=[
                pl.BlockSpec((cols, wide, observations), whole),
                pl.BlockSpec((cols, patch_rows, observations), shifted),
                pl.BlockSpec((cols, patch_rows, observations), shifted),
                pl.BlockSpec((1, wide, lanes), lambda c, me: (c + base, 0, 0)),
                pl.BlockSpec((tracers, height, wide, PLON), lambda c, me: (0, 0, 0, c)),
            ],
            out_specs=[pl.BlockSpec((group, tracers, own, PLON), lambda c, me: (0, 0, 0, c))]
            * groups
            + [pl.BlockSpec((1, block, lanes), lambda c, me: (c, 0, 0))] * groups,
            scratch_shapes=[
                pltpu.VMEM((cols, wide, wide), f32),
                pltpu.VMEM((cols, wide, wide), f32),
                pltpu.VMEM((PLON // LANES, members, own, LANES), f32),
            ],
        ),
        out_shape=[jax.ShapeDtypeStruct((group, tracers, own, longitudes), bf16)] * groups
        + [jax.ShapeDtypeStruct((cols, block, lanes), bf16)] * groups,
        compiler_params=pltpu.CompilerParams(vmem_limit_bytes=60 * 2**20),
        cost_estimate=pl.CostEstimate(
            flops=6 * 10**9, bytes_accessed=8 * tracers * height * wide * longitudes, transcendentals=0
        ),
        name="analysis",
    )(me, seen.reshape(cols, wide, observations), measured, variance, theta, bg)


def assemble_kernel(groups, first, lanes, me_ref, *refs):
    pieces = refs[:groups]
    out = refs[groups + (0 if first else 1)]
    buffer, arrived, left = refs[-3:]
    own = pieces[0].shape[2]
    ins, outs = [], []
    for j in range(groups):
        ins.append(pltpu.make_async_copy(pieces[j], buffer.at[j], arrived.at[j]))
        ins[j].start()
    for j in range(groups):
        start = pl.multiple_of((me_ref[0] ^ j) * own, own)
        ins[j].wait()
        outs.append(
            pltpu.make_async_copy(
                buffer.at[j], out.at[:, :, pl.ds(start, own), lanes], left.at[j]
            )
        )
        outs[j].start()
    for j in range(groups):
        outs[j].wait()


def assemble(me, pieces, before, start, shape):
    groups = len(pieces)
    width = pieces[0].shape[-1]
    any_spec = pl.BlockSpec(memory_space=pl.ANY)
    extra = [] if before is None else [before]
    return pl.pallas_call(
        functools.partial(assemble_kernel, groups, before is None, pl.ds(start, width)),
        grid_spec=pltpu.PrefetchScalarGridSpec(
            num_scalar_prefetch=1,
            grid=(1,),
            in_specs=[any_spec] * (groups + len(extra)),
            out_specs=any_spec,
            scratch_shapes=[
                pltpu.VMEM((groups,) + pieces[0].shape, bf16),
                pltpu.SemaphoreType.DMA((groups,)),
                pltpu.SemaphoreType.DMA((groups,)),
            ],
        ),
        out_shape=jax.ShapeDtypeStruct(shape, bf16),
        input_output_aliases={} if before is None else {groups + 1: 0},
        compiler_params=pltpu.CompilerParams(vmem_limit_bytes=40 * 2**20),
        cost_estimate=pl.CostEstimate(
            flops=0, bytes_accessed=2 * 2 * groups * math.prod(pieces[0].shape), transcendentals=0
        ),
        name="assemble",
    )(me, *pieces, *extra)


def on_device(
    initial_concentrations,
    rate_field,
    kinetic_scaling_factors,
    observed_cell,
    measured_value,
    error_variance,
):
    group, tracers, band, longitudes = initial_concentrations.shape
    bands = lax.axis_size("grid")
    groups = lax.axis_size("mem")
    members = group * groups
    reactions = rate_field.shape[0]
    waves = NW // bands
    latitudes = band * bands
    own = band // groups
    patch_rows = own // PLAT
    cols = longitudes // PLON
    mem = lax.axis_index("mem")

    place_on_grid = lax.axis_index("grid").astype(jnp.int32).reshape(1)
    fourier = forward_transform(place_on_grid, initial_concentrations, bands, waves)
    arrived = []
    for k, piece in enumerate(fourier):
        pairs = [(i, i ^ k) for i in range(bands)]
        arrived.append(piece if k == 0 else lax.ppermute(piece, "grid", pairs))

    factors = lax.all_to_all(
        kinetic_scaling_factors.reshape(group, reactions, groups, patch_rows, cols).transpose(
            2, 0, 1, 3, 4
        ),
        "mem",
        split_axis=0,
        concat_axis=0,
        tiled=True,
    ).reshape(members, reactions, patch_rows, cols)
    ahead, back = meridional_tables(latitudes, own, bands, groups)
    gain = spectral_gain(latitudes, waves, bands)
    inverse = inverse_table(longitudes, waves, bands)
    rate = (
        lax.dynamic_slice_in_dim(rate_field, mem * own, own, 1)
        .astype(f32)
        .reshape(reactions, patch_rows, PLAT, longitudes)
        .transpose(0, 2, 1, 3)
    )
    factor = jnp.broadcast_to(
        factors.astype(f32).transpose(3, 0, 1, 2)[..., None],
        (cols, members, reactions, patch_rows, LANES),
    )

    def own_patches(array):
        mine = lax.dynamic_slice_in_dim(array, mem * patch_rows, patch_rows, 0)
        return mine.transpose(1, 0, 2)

    cell = own_patches(observed_cell)
    lane = cell % PLON
    place = cell // PLON
    observed = own_patches(measured_value)
    variance = own_patches(error_variance)

    last = meridional_transform(
        arrived,
        ahead,
        back,
        gain,
        waves,
        tracers,
        groups * bands,
    )
    returned = lax.all_to_all(last, ("mem", "grid"), split_axis=0, concat_axis=0, tiled=True)
    z = returned.reshape(groups, bands, group * tracers * own, 2 * waves)
    me = mem.astype(jnp.int32).reshape(1)
    theta = jnp.pad(
        jnp.log(factors.astype(f32)).transpose(3, 0, 2, 1),
        ((0, 0), (0, 0), (0, 0), (0, LANES - reactions)),
    ).reshape(cols, members * patch_rows, LANES)

    chunks = CHUNKS if cols % CHUNKS == 0 else 1
    per = cols // chunks
    landed, updated = [], []
    for chunk in range(chunks):
        base = chunk * per
        bg, seen = chemistry(z, inverse, rate, factor, lane, place, tracers, base, per)
        results = analyse(me, seen, observed, variance, theta, bg, base, groups, own)
        if chunk < chunks - 1:
            z, results = lax.optimization_barrier((z, results))
        sent = []
        for j, result in enumerate(results):
            pairs = [(i, i ^ (j % groups)) for i in range(groups)]
            sent.append(result if j % groups == 0 else lax.ppermute(result, "mem", pairs))
        landed.append(sent[:groups])
        updated.append(sent[groups:])

    shape = (group, tracers, band, longitudes)
    order = mem ^ jnp.arange(groups, dtype=jnp.int32)
    if own % SUBLANES == 0:
        analysis = None
        for chunk in range(chunks):
            analysis = assemble(me, landed[chunk], analysis, chunk * per * PLON, shape)
    else:
        joined = jnp.stack(
            [jnp.concatenate([part[j] for part in landed], axis=-1) for j in range(groups)]
        )
        joined = jnp.take(joined, order, axis=0)
        analysis = joined.transpose(1, 2, 0, 3, 4).reshape(shape)
    fresh = jnp.stack([jnp.concatenate([part[j] for part in updated]) for j in range(groups)])
    fresh = fresh[..., :reactions].reshape(groups, cols, group, patch_rows, reactions)
    mine = (order[:, None] == jnp.arange(groups, dtype=jnp.int32)[None, :]).astype(bf16)
    mult_analysis = jnp.einsum(
        "jr,jcgpa->garpc", mine, fresh, preferred_element_type=f32
    ).astype(bf16)
    mult_analysis = mult_analysis.reshape(group, reactions, groups * patch_rows, cols)
    return (analysis, mult_analysis)


def solution(mesh):
    return jax.shard_map(
        on_device,
        mesh=mesh,
        in_specs=(
            P("mem", None, "grid", None),
            P(None, "grid", None),
            P("mem", None, "grid", None),
            P("grid", None, None),
            P("grid", None, None),
            P("grid", None, None),
        ),
        out_specs=(P("mem", None, "grid", None), P("mem", None, "grid", None)),
        check_vma=False,
    )
```

```python
import functools
import math

import jax
import jax.numpy as jnp
from jax import lax
from jax.experimental import pallas as pl
from jax.experimental.pallas import tpu as pltpu
from jax.sharding import PartitionSpec as P

NW = 512
PLAT = 3
PLON = 256
SWEEPS = 5
LANES = 128
SUBLANES = 8
CHUNKS = 3
HALVES = 2


damping = 2.0
f32 = jnp.float32
bf16 = jnp.bfloat16


def rounded_angle(product, period):
    turns = jnp.floor(product * (1.0 / period))
    return (product - turns * period) * (2.0 * math.pi / period)


def forward_kernel(bands, waves, me_ref, x_ref, *refs):
    outs = refs[:bands]
    table, coarse, fine = refs[bands:]
    tracers, band, longitudes = x_ref.shape[1:]
    columns = table.shape[1]
    local = 2 * waves
    step = fine.shape[1]

    @pl.when(pl.program_id(0) == 0)
    def _():
        def waves_of(rows):
            q = lax.broadcasted_iota(jnp.int32, (rows, columns), 1)
            p = (q // local) ^ me_ref[0]
            part = (q % local) // waves
            wave = bands * (q % waves) + p
            return wave.astype(f32), part

        rows = coarse.shape[1]
        wave, part = waves_of(rows)
        row = lax.broadcasted_iota(jnp.int32, (rows, columns), 0) * step
        angle = rounded_angle(wave * row.astype(f32), longitudes)
        cosine, sine = jnp.cos(angle), jnp.sin(angle)
        coarse[0] = jnp.where(part == 0, cosine, -sine)
        coarse[1] = jnp.where(part == 0, sine, cosine)
        wave, part = waves_of(step)
        row = lax.broadcasted_iota(jnp.int32, (step, columns), 0)
        angle = rounded_angle(wave * row.astype(f32), longitudes)
        fine[0] = jnp.cos(angle)
        fine[1] = jnp.sin(angle)

        def build(at, carry):
            block = coarse[0, pl.ds(at, 1), :] * fine[0] - coarse[1, pl.ds(at, 1), :] * fine[1]
            start = pl.multiple_of(at * step, step)
            table[pl.ds(start, step), :] = block.astype(bf16)
            return carry

        lax.fori_loop(0, rows, build, 0)

    x = x_ref[0].astype(bf16).reshape(tracers * band, longitudes)
    y = jnp.dot(x, table[...], preferred_element_type=f32) * (1.0 / longitudes)
    y = y.astype(bf16).reshape(tracers, band, columns)
    for t in range(tracers):
        for k in range(bands):
            outs[k][:, t * local : (t + 1) * local] = y[t, :, k * local : (k + 1) * local]


def forward_transform(me, x, bands, waves, first, group):
    _, tracers, band, longitudes = x.shape
    local = 2 * waves
    step = 32 if longitudes % 32 == 0 else 8
    return pl.pallas_call(
        functools.partial(forward_kernel, bands, waves),
        grid_spec=pltpu.PrefetchScalarGridSpec(
            num_scalar_prefetch=1,
            grid=(group,),
            in_specs=[
                pl.BlockSpec((1, tracers, band, longitudes), lambda g, me: (g + first, 0, 0, 0))
            ],
            out_specs=[pl.BlockSpec((band, tracers * local), lambda g, me: (0, g))] * bands,
            scratch_shapes=[
                pltpu.VMEM((longitudes, bands * local), bf16),
                pltpu.VMEM((2, longitudes // step, bands * local), f32),
                pltpu.VMEM((2, step, bands * local), f32),
            ],
        ),
        out_shape=[jax.ShapeDtypeStruct((band, group * tracers * local), bf16)] * bands,
        compiler_params=pltpu.CompilerParams(vmem_limit_bytes=60 * 2**20),
        cost_estimate=pl.CostEstimate(
            flops=2 * group * tracers * band * longitudes * bands * local,
            bytes_accessed=4 * group * tracers * band * longitudes,
            transcendentals=0,
        ),
        name="forward_dft",
    )(me, x)


def meridional_kernel(waves, bands, *refs):
    pieces = refs[:bands]
    ahead_ref, back_ref, gain_ref = refs[bands : bands + 3]
    o_ref, arrived = refs[-2:]
    local = 2 * waves
    band, columns = pieces[0].shape
    tracers = columns // local
    for k in range(bands):
        arrived[k * band : (k + 1) * band, :] = pieces[k][...]
    spectrum = jnp.dot(ahead_ref[...], arrived[...], preferred_element_type=f32)
    gain = jnp.concatenate([gain_ref[...]] * tracers, axis=1)
    damped = (spectrum * gain).astype(bf16)
    back = jnp.dot(back_ref[...], damped, preferred_element_type=f32).astype(bf16)
    owners, _, rows, _ = o_ref.shape
    own = rows // tracers
    for t in range(tracers):
        part = back[:, t * local : (t + 1) * local].reshape(owners, own, local)
        o_ref[:, 0, t * own : (t + 1) * own, :] = part


def meridional_transform(arrived, ahead, back, gain, waves, tracers, owners, before, first, group):
    band, columns = arrived[0].shape
    bands = len(arrived)
    latitudes = bands * band
    local = 2 * waves
    own = latitudes // owners
    whole = lambda g: (0, 0)
    extra = [] if before is None else [before]
    return pl.pallas_call(
        functools.partial(meridional_kernel, waves, bands),
        grid=(columns // (tracers * local),),
        in_specs=[pl.BlockSpec((band, tracers * local), lambda g: (0, g))] * bands
        + [
            pl.BlockSpec(ahead.shape, whole),
            pl.BlockSpec(back.shape, whole),
            pl.BlockSpec(gain.shape, whole),
        ]
        + [pl.BlockSpec(memory_space=pl.ANY)] * len(extra),
        out_specs=pl.BlockSpec((owners, 1, tracers * own, local), lambda g: (0, g + first, 0, 0)),
        out_shape=jax.ShapeDtypeStruct((owners, group, tracers * own, local), bf16),
        compiler_params=pltpu.CompilerParams(vmem_limit_bytes=60 * 2**20),
        input_output_aliases={} if before is None else {bands + 3: 0},
        scratch_shapes=[pltpu.VMEM((latitudes, tracers * local), bf16)],
        cost_estimate=pl.CostEstimate(
            flops=4 * latitudes * NW * columns,
            bytes_accessed=4 * latitudes * columns,
            transcendentals=0,
        ),
        name="meridional",
    )(*arrived, ahead, back, gain, *extra)


def meridional_tables(latitudes, own, bands, groups):
    device = lax.axis_index("grid")
    even = device % 2 == 0
    modes = jnp.arange(NW, dtype=jnp.int32)
    order = jnp.where(even, modes, modes + 1).astype(f32)

    def values(theta, order):
        angle = theta * order
        return jnp.where(even, jnp.cos(angle), jnp.sin(angle)).astype(bf16)

    band = own * groups
    lat = jnp.arange(latitudes, dtype=jnp.int32)
    lat = ((lat // band) ^ device) * band + lat % band
    theta = (lat.astype(f32) + 0.5) * (math.pi / latitudes)
    ahead = values(theta[None, :], order[:, None])
    rows = own // PLAT
    index = (
        lax.broadcasted_iota(jnp.int32, (groups, bands, PLAT, rows), 0) * own
        + lax.broadcasted_iota(jnp.int32, (groups, bands, PLAT, rows), 1) * (own * groups)
        + lax.broadcasted_iota(jnp.int32, (groups, bands, PLAT, rows), 2)
        + lax.broadcasted_iota(jnp.int32, (groups, bands, PLAT, rows), 3) * PLAT
    ).reshape(latitudes)
    theta = (index.astype(f32) + 0.5) * (math.pi / latitudes)
    back = values(theta[:, None], order[None, :])
    return ahead, back


def spectral_gain(latitudes, waves, bands):
    device = lax.axis_index("grid")
    modes = jnp.arange(NW, dtype=jnp.int32)[:, None]
    column = jnp.arange(2 * waves, dtype=jnp.int32)[None, :]
    wave = bands * (column % waves) + device
    total = (wave + modes).astype(f32)
    ratio = total * (total + 1.0) / float(NW * (NW - 1))
    half = jnp.where((wave % 2 == 0) & (modes == 0), 0.5, 1.0)
    gain = half / (1.0 + damping * ratio * ratio)
    return jnp.where(wave + modes <= NW - 1, gain, 0.0) * (2.0 / latitudes)


def inverse_table(longitudes, waves, bands):
    q = jnp.arange(bands * 2 * waves, dtype=jnp.int32)
    device = q // (2 * waves)
    part = (q % (2 * waves)) // waves
    wave = bands * (q % waves) + device
    column = jnp.arange(longitudes, dtype=jnp.int32)
    phase = wave[:, None] * column[None, :] % longitudes
    phase = phase + jnp.where(part == 0, 0, longitudes // 4)[:, None]
    weight = jnp.where(wave == 0, 1.0, 2.0)[:, None]
    angle = phase.astype(f32) * (2.0 * math.pi / longitudes)
    return (weight * jnp.cos(angle)).astype(bf16)


def chemistry_kernel(
    z_ref, table_ref, rate_ref, factor_ref, lane_ref, place_ref, bg_ref, seen_ref, lhs, smooth, fresh
):
    sources, bands, rows, local = z_ref.shape
    reactions, height, patch_rows, _ = rate_ref.shape
    members = factor_ref.shape[1]
    tracers = bg_ref.shape[0]
    others = tracers - 1

    @pl.when(pl.program_id(0) == 0)
    def _():
        for s in range(sources):
            for p in range(bands):
                lhs[s * rows : (s + 1) * rows, p * local : (p + 1) * local] = z_ref[s, p]

    smooth[...] = jnp.dot(lhs[...], table_ref[...], preferred_element_type=f32).reshape(
        members, tracers, height, patch_rows, PLON
    )

    def one_member(e, carry):
        for i in range(height):
            for at in range(0, PLON, LANES):
                lanes = slice(at, at + LANES)
                rates = [
                    factor_ref[0, e, r] * rate_ref[r, i, :, lanes] for r in range(reactions)
                ]
                kept = []
                for a in range(tracers):
                    outflow = rates[others * a]
                    for s in range(1, others):
                        outflow = outflow + rates[others * a + s]
                    kept.append(smooth[e, a, i, :, lanes] * (1.0 / (1.0 + outflow)))
                for b in range(tracers):
                    value = kept[b]
                    for a in range(tracers):
                        if a != b:
                            s = b if b < a else b - 1
                            value = value + rates[others * a + s] * kept[a]
                    fresh[b, i, e, :, lanes] = value
        return carry

    lax.fori_loop(0, members, one_member, 0)
    for t in range(tracers):
        for i in range(height):
            bg_ref[t, i] = fresh[t, i].reshape(members * patch_rows, PLON).astype(bf16)

    copies = max(1, SUBLANES // patch_rows)

    def tiled(array):
        return jnp.concatenate([array] * copies, axis=0) if copies > 1 else array

    lane = tiled(lane_ref[0])
    place = tiled(place_ref[0])
    within = lane % LANES
    piece = lane // LANES

    def observe(e, carry):
        seen = jnp.zeros(lane.shape, f32)
        for t in range(tracers):
            for i in range(height):
                value = tiled(fresh[t, i, e])
                for k in range(PLON // LANES):
                    found = jnp.take_along_axis(
                        value[:, k * LANES : (k + 1) * LANES],
                        within,
                        axis=1,
                        mode="promise_in_bounds",
                    )
                    here = (place == t * height + i) & (piece == k)
                    seen = jnp.where(here, found, seen)
        seen_ref[0, e] = seen[:patch_rows].astype(bf16).astype(f32)
        return carry

    lax.fori_loop(0, members, observe, 0)


def chemistry(z, table, rate, factor, lane, place, tracers, base, cols):
    sources, bands, rows, local = z.shape
    reactions, height, patch_rows, _ = rate.shape
    members = factor.shape[1]
    observations = lane.shape[-1]
    return pl.pallas_call(
        chemistry_kernel,
        grid=(cols,),
        in_specs=[
            pl.BlockSpec(z.shape, lambda c: (0, 0, 0, 0)),
            pl.BlockSpec((table.shape[0], PLON), lambda c: (0, c + base)),
            pl.BlockSpec((reactions, height, patch_rows, PLON), lambda c: (0, 0, 0, c + base)),
            pl.BlockSpec((1, members, reactions, patch_rows, LANES), lambda c: (c + base, 0, 0, 0, 0)),
            pl.BlockSpec((1, patch_rows, observations), lambda c: (c + base, 0, 0)),
            pl.BlockSpec((1, patch_rows, observations), lambda c: (c + base, 0, 0)),
        ],
        out_specs=[
            pl.BlockSpec((tracers, height, members * patch_rows, PLON), lambda c: (0, 0, 0, c)),
            pl.BlockSpec((1, members, patch_rows, observations), lambda c: (c, 0, 0, 0)),
        ],
        out_shape=[
            jax.ShapeDtypeStruct((tracers, height, members * patch_rows, cols * PLON), bf16),
            jax.ShapeDtypeStruct((cols, members, patch_rows, observations), f32),
        ],
        scratch_shapes=[
            pltpu.VMEM((sources * rows, bands * local), bf16),
            pltpu.VMEM((members, tracers, height, patch_rows, PLON), f32),
            pltpu.VMEM((tracers, height, members, patch_rows, PLON), f32),
        ],
        compiler_params=pltpu.CompilerParams(vmem_limit_bytes=60 * 2**20),
        cost_estimate=pl.CostEstimate(
            flops=2 * sources * rows * bands * local * cols * PLON,
            bytes_accessed=2 * math.prod(z.shape) * 8,
            transcendentals=0,
        ),
        name="chemistry",
    )(z, table, rate, factor, lane, place)


def precise_dot(a, b):
    return jnp.dot(a, b, preferred_element_type=f32, precision=lax.Precision.HIGHEST)


def member_weights(seen, measured, variance, members, patch_rows):
    wide = members * patch_rows
    row = lax.broadcasted_iota(jnp.int32, (wide, wide), 0)
    column = lax.broadcasted_iota(jnp.int32, (wide, wide), 1)
    mask = (row % patch_rows == column % patch_rows).astype(f32)
    identity = (row == column).astype(f32)
    spare = members - 1.0

    def over_members(array):
        return jnp.sum(array.reshape(members, patch_rows, array.shape[-1]), axis=0)

    def each_member(array):
        return jnp.concatenate([array] * members, axis=0)

    currents, scales, projections = [], [], []
    for predicted, observed, errors in zip(seen, measured, variance):
        mean = over_members(predicted) * (1.0 / members)
        spread = predicted - each_member(mean)
        weighted = spread * each_member(1.0 / errors)
        outer = mask * lax.dot_general(
            weighted,
            spread,
            (((1,), (1,)), ((), ())),
            preferred_element_type=f32,
            precision=lax.Precision.HIGHEST,
        )
        square = over_members(jnp.sum(outer * outer, axis=1, keepdims=True))
        scale = each_member(spare + jnp.sqrt(square))
        currents.append((spare * identity + outer) * (1.0 / scale))
        scales.append(scale)
        innovation = each_member(observed - mean)
        projections.append(jnp.sum(weighted * innovation, axis=1, keepdims=True))

    roots = [1.5 * identity - 0.5 * current for current in currents]
    currents = [precise_dot(c, m) for c, m in zip(currents, roots)]
    for sweep in range(1, SWEEPS):
        middles = [
            1.5 * identity - 0.5 * precise_dot(r, c) for r, c in zip(roots, currents)
        ]
        if sweep < SWEEPS - 1:
            currents = [precise_dot(c, m) for c, m in zip(currents, middles)]
        roots = [precise_dot(m, r) for m, r in zip(middles, roots)]

    weights = []
    for root, scale, projected in zip(roots, scales, projections):
        along = jnp.sum(identity * projected, axis=0, keepdims=True)
        once = jnp.sum(root * along, axis=1, keepdims=True)
        twice = jnp.sum(root * (once * (1.0 / scale)), axis=0, keepdims=True)
        transform = jnp.sqrt(spare / scale) * root + mask * twice
        rest = (1.0 - jnp.sum(transform, axis=1, keepdims=True)) * (1.0 / members)
        weights.append(transform + mask * rest)
    return weights


def analysis_kernel(groups, me_ref, seen_ref, measured_ref, variance_ref, theta_ref, bg_ref, *refs):
    outs, factors = refs[:groups], refs[groups : 2 * groups]
    high, low, rows = refs[2 * groups :]
    cols, patch_rows, _ = measured_ref.shape
    group, tracers, own, _ = outs[0].shape
    members = groups * group
    height = own // patch_rows
    block = group * patch_rows
    at = pl.program_id(0)

    @pl.when(at == 0)
    def _():
        weights = member_weights(
            [seen_ref[c] for c in range(cols)],
            [measured_ref[c] for c in range(cols)],
            [variance_ref[c] for c in range(cols)],
            members,
            patch_rows,
        )
        for c in range(cols):
            upper = weights[c].astype(bf16)
            high[c] = weights[c]
            low[c] = weights[c] - upper.astype(f32)

    def by_partner(ref):
        parts = []
        for j in range(groups):
            start = pl.multiple_of((me_ref[0] ^ j) * block, block)
            parts.append(ref[at, pl.ds(start, block), :])
        return jnp.concatenate(parts, axis=0)

    exact = by_partner(high)
    updated = jnp.exp(precise_dot(exact, theta_ref[0])).astype(bf16)
    for j in range(groups):
        factors[j][0] = updated[j * block : (j + 1) * block]
    upper = exact.astype(bf16)
    lower = by_partner(low).astype(bf16)
    for t in range(tracers):
        for i in range(height):
            value = bg_ref[t, i]
            new = jnp.dot(upper, value, preferred_element_type=f32)
            new = new + jnp.dot(lower, value, preferred_element_type=f32)
            for e in range(members):
                part = new[e * patch_rows : (e + 1) * patch_rows]
                for k in range(PLON // LANES):
                    rows[k, e, pl.ds(i, patch_rows, stride=height), :] = part[
                        :, k * LANES : (k + 1) * LANES
                    ]
        for j in range(groups):
            for k in range(PLON // LANES):
                outs[j][:, t, :, k * LANES : (k + 1) * LANES] = rows[
                    k, j * group : (j + 1) * group
                ].astype(bf16)


def analyse(me, seen, measured, variance, theta, bg, base, groups, own):
    cols, members, patch_rows, observations = seen.shape
    group = members // groups
    tracers, height, wide, longitudes = bg.shape
    block = group * patch_rows
    lanes = theta.shape[-1]
    whole = lambda c, me: (0, 0, 0)
    shifted = lambda c, me: (base // cols, 0, 0)
    return pl.pallas_call(
        functools.partial(analysis_kernel, groups),
        grid_spec=pltpu.PrefetchScalarGridSpec(
            num_scalar_prefetch=1,
            grid=(cols,),
            in_specs=[
                pl.BlockSpec((cols, wide, observations), whole),
                pl.BlockSpec((cols, patch_rows, observations), shifted),
                pl.BlockSpec((cols, patch_rows, observations), shifted),
                pl.BlockSpec((1, wide, lanes), lambda c, me: (c + base, 0, 0)),
                pl.BlockSpec((tracers, height, wide, PLON), lambda c, me: (0, 0, 0, c)),
            ],
            out_specs=[pl.BlockSpec((group, tracers, own, PLON), lambda c, me: (0, 0, 0, c))]
            * groups
            + [pl.BlockSpec((1, block, lanes), lambda c, me: (c, 0, 0))] * groups,
            scratch_shapes=[
                pltpu.VMEM((cols, wide, wide), f32),
                pltpu.VMEM((cols, wide, wide), f32),
                pltpu.VMEM((PLON // LANES, members, own, LANES), f32),
            ],
        ),
        out_shape=[jax.ShapeDtypeStruct((group, tracers, own, longitudes), bf16)] * groups
        + [jax.ShapeDtypeStruct((cols, block, lanes), bf16)] * groups,
        compiler_params=pltpu.CompilerParams(vmem_limit_bytes=60 * 2**20),
        cost_estimate=pl.CostEstimate(
            flops=6 * 10**9, bytes_accessed=8 * tracers * height * wide * longitudes, transcendentals=0
        ),
        name="analysis",
    )(me, seen.reshape(cols, wide, observations), measured, variance, theta, bg)


def assemble_kernel(groups, first, lanes, me_ref, *refs):
    pieces = refs[:groups]
    out = refs[groups + (0 if first else 1)]
    buffer, arrived, left = refs[-3:]
    own = pieces[0].shape[2]
    ins, outs = [], []
    for j in range(groups):
        ins.append(pltpu.make_async_copy(pieces[j], buffer.at[j], arrived.at[j]))
        ins[j].start()
    for j in range(groups):
        start = pl.multiple_of((me_ref[0] ^ j) * own, own)
        ins[j].wait()
        outs.append(
            pltpu.make_async_copy(
                buffer.at[j], out.at[:, :, pl.ds(start, own), lanes], left.at[j]
            )
        )
        outs[j].start()
    for j in range(groups):
        outs[j].wait()


def assemble(me, pieces, before, start, shape):
    groups = len(pieces)
    width = pieces[0].shape[-1]
    any_spec = pl.BlockSpec(memory_space=pl.ANY)
    extra = [] if before is None else [before]
    return pl.pallas_call(
        functools.partial(assemble_kernel, groups, before is None, pl.ds(start, width)),
        grid_spec=pltpu.PrefetchScalarGridSpec(
            num_scalar_prefetch=1,
            grid=(1,),
            in_specs=[any_spec] * (groups + len(extra)),
            out_specs=any_spec,
            scratch_shapes=[
                pltpu.VMEM((groups,) + pieces[0].shape, bf16),
                pltpu.SemaphoreType.DMA((groups,)),
                pltpu.SemaphoreType.DMA((groups,)),
            ],
        ),
        out_shape=jax.ShapeDtypeStruct(shape, bf16),
        input_output_aliases={} if before is None else {groups + 1: 0},
        compiler_params=pltpu.CompilerParams(vmem_limit_bytes=40 * 2**20),
        cost_estimate=pl.CostEstimate(
            flops=0, bytes_accessed=2 * 2 * groups * math.prod(pieces[0].shape), transcendentals=0
        ),
        name="assemble",
    )(me, *pieces, *extra)


def on_device(
    initial_concentrations,
    rate_field,
    kinetic_scaling_factors,
    observed_cell,
    measured_value,
    error_variance,
):
    group, tracers, band, longitudes = initial_concentrations.shape
    bands = lax.axis_size("grid")
    groups = lax.axis_size("mem")
    members = group * groups
    reactions = rate_field.shape[0]
    waves = NW // bands
    latitudes = band * bands
    own = band // groups
    patch_rows = own // PLAT
    cols = longitudes // PLON
    mem = lax.axis_index("mem")

    place_on_grid = lax.axis_index("grid").astype(jnp.int32).reshape(1)
    place_on_grid = lax.axis_index("grid").astype(jnp.int32).reshape(1)
    halves = HALVES if group % HALVES == 0 else 1
    part = group // halves
    arrived = []
    for half in range(halves):
        fourier = forward_transform(
            place_on_grid, initial_concentrations, bands, waves, half * part, part
        )
        pieces = []
        for k, piece in enumerate(fourier):
            pairs = [(i, i ^ k) for i in range(bands)]
            pieces.append(piece if k == 0 else lax.ppermute(piece, "grid", pairs))
        arrived.append(pieces)
        if half < halves - 1:
            initial_concentrations, arrived[-1][0] = lax.optimization_barrier(
                (initial_concentrations, arrived[-1][0])
            )

    factors = lax.all_to_all(
        kinetic_scaling_factors.reshape(group, reactions, groups, patch_rows, cols).transpose(
            2, 0, 1, 3, 4
        ),
        "mem",
        split_axis=0,
        concat_axis=0,
        tiled=True,
    ).reshape(members, reactions, patch_rows, cols)
    ahead, back = meridional_tables(latitudes, own, bands, groups)
    gain = spectral_gain(latitudes, waves, bands)
    inverse = inverse_table(longitudes, waves, bands)
    rate = (
        lax.dynamic_slice_in_dim(rate_field, mem * own, own, 1)
        .astype(f32)
        .reshape(reactions, patch_rows, PLAT, longitudes)
        .transpose(0, 2, 1, 3)
    )
    factor = jnp.broadcast_to(
        factors.astype(f32).transpose(3, 0, 1, 2)[..., None],
        (cols, members, reactions, patch_rows, LANES),
    )

    def own_patches(array):
        mine = lax.dynamic_slice_in_dim(array, mem * patch_rows, patch_rows, 0)
        return mine.transpose(1, 0, 2)

    cell = own_patches(observed_cell)
    lane = cell % PLON
    place = cell // PLON
    observed = own_patches(measured_value)
    variance = own_patches(error_variance)

    last = None
    for half in range(halves):
        last = meridional_transform(
            arrived[half],
            ahead,
            back,
            gain,
            waves,
            tracers,
            groups * bands,
            last,
            half * part,
            group,
        )
    returned = lax.all_to_all(last, ("mem", "grid"), split_axis=0, concat_axis=0, tiled=True)
    z = returned.reshape(groups, bands, group * tracers * own, 2 * waves)
    me = mem.astype(jnp.int32).reshape(1)
    theta = jnp.pad(
        jnp.log(factors.astype(f32)).transpose(3, 0, 2, 1),
        ((0, 0), (0, 0), (0, 0), (0, LANES - reactions)),
    ).reshape(cols, members * patch_rows, LANES)

    chunks = CHUNKS if cols % CHUNKS == 0 else 1
    per = cols // chunks
    landed, updated = [], []
    for chunk in range(chunks):
        base = chunk * per
        bg, seen = chemistry(z, inverse, rate, factor, lane, place, tracers, base, per)
        results = analyse(me, seen, observed, variance, theta, bg, base, groups, own)
        if chunk < chunks - 1:
            z, results = lax.optimization_barrier((z, results))
        sent = []
        for j, result in enumerate(results):
            pairs = [(i, i ^ (j % groups)) for i in range(groups)]
            sent.append(result if j % groups == 0 else lax.ppermute(result, "mem", pairs))
        landed.append(sent[:groups])
        updated.append(sent[groups:])

    shape = (group, tracers, band, longitudes)
    order = mem ^ jnp.arange(groups, dtype=jnp.int32)
    if own % SUBLANES == 0:
        analysis = None
        for chunk in range(chunks):
            analysis = assemble(me, landed[chunk], analysis, chunk * per * PLON, shape)
    else:
        joined = jnp.stack(
            [jnp.concatenate([part[j] for part in landed], axis=-1) for j in range(groups)]
        )
        joined = jnp.take(joined, order, axis=0)
        analysis = joined.transpose(1, 2, 0, 3, 4).reshape(shape)
    fresh = jnp.stack([jnp.concatenate([part[j] for part in updated]) for j in range(groups)])
    fresh = fresh[..., :reactions].reshape(groups, cols, group, patch_rows, reactions)
    mine = (order[:, None] == jnp.arange(groups, dtype=jnp.int32)[None, :]).astype(bf16)
    mult_analysis = jnp.einsum(
        "jr,jcgpa->garpc", mine, fresh, preferred_element_type=f32
    ).astype(bf16)
    mult_analysis = mult_analysis.reshape(group, reactions, groups * patch_rows, cols)
    return (analysis, mult_analysis)


def solution(mesh):
    return jax.shard_map(
        on_device,
        mesh=mesh,
        in_specs=(
            P("mem", None, "grid", None),
            P(None, "grid", None),
            P("mem", None, "grid", None),
            P("grid", None, None),
            P("grid", None, None),
            P("grid", None, None),
        ),
        out_specs=(P("mem", None, "grid", None), P("mem", None, "grid", None)),
        check_vma=False,
    )
```
